32 devices in a mesh: dp: 4 (over y, x), seq: 8 (over z, core).
Axes of the slice: x: 2, y: 2, z: 4, core: 2. Of those that a mesh axis runs over, the one named last changes fastest.
Arguments:
- tokens: bfloat16 [4, 2352, 1536], P('dp', 'seq'), may hold values from -6 to 6
- condition: float32 [4, 1024], P(None, ('dp', 'seq')), may hold values from -6 to 6
- caption: bfloat16 [4, 256, 4096], P(None, None, ('dp', 'seq')), may hold values from -6 to 6
- caption_len: int32 [4], replicated, may hold values from 1 to 256, as said below
- image_shape: int32 [4, 2], replicated, may hold values from 12 to 48, as said below
- cotangent: bfloat16 [4, 2352, 1536], P('dp', 'seq'), may hold values from -6 to 6
- joint_weight: bfloat16 [1536, 4608], P(('dp', 'seq')), may hold values from -0.15625 to 0.15625
- mixer_weight: bfloat16 [1536, 1536], P(('dp', 'seq')), may hold values from -0.15625 to 0.15625
- gate_up_weight: bfloat16 [1536, 8192], P(('dp', 'seq')), may hold values from -0.15625 to 0.15625
- down_weight: bfloat16 [4096, 1536], P(('dp', 'seq')), may hold values from -0.09375 to 0.09375
- text_weight: bfloat16 [4096, 3072], P(('dp', 'seq')), may hold values from -0.09375 to 0.09375
- modulation_weight: bfloat16 [1024, 9216], P(('dp', 'seq')), may hold values from -0.1875 to 0.1875
- modulation_bias: float32 [9216], P(('dp', 'seq')), may hold values from -3 to 3
- norm_gains: bfloat16 [7, 1536], P(None, ('dp', 'seq')), may hold values from 0.25 to 1.75
- head_gates: float32 [24], replicated, may hold values from -1.5 to 1.5
Outputs:
- output: bfloat16 [4, 2352, 1536], P('dp', 'seq')
- tokens_grad: bfloat16 [4, 2352, 1536], P('dp', 'seq')
- joint_grad: float32 [1536, 4608], P(('dp', 'seq'))
- mixer_grad: float32 [1536, 1536], P(('dp', 'seq'))
- gate_up_grad: float32 [1536, 8192], P(('dp', 'seq'))
- down_grad: float32 [4096, 1536], P(('dp', 'seq'))
- text_grad: float32 [4096, 3072], P(('dp', 'seq'))
- modulation_grad: float32 [1024, 9216], P(('dp', 'seq'))
- bias_grad: float32 [9216], P(('dp', 'seq'))
- gains_grad: float32 [7, 1536], P(None, ('dp', 'seq'))
- gates_grad: float32 [24], replicated
The draws below stay inside these ranges and needn't reach their ends.
Inputs may be any that keep to these rules, and one draw needn't show every extreme that they name: `caption_len`: text tokens at or beyond an item's caption length are padding; some item's caption has all 256 tokens in every draw. `image_shape`: row (height, width) of an item: its first height * (width + 1) tokens are height image rows of width tokens, each followed by a nextline marker, and the tokens after them are padding; height >= 24; some item has height = width = 48 in every draw.
All inputs are finite; a program needn't handle non-finite values.
Results may differ from the reference program's by a relative error of at most 0.04.
Values may be sent and summed in bfloat16 or wider, within the bound.
No kernel may reach another device: no remote copies, remote signals or barrier semaphores. Data moves between devices by JAX's collectives and lax.ppermute only.
A program may use at most 448 MiB of HBM per device.

```python
import jax
import jax.numpy as jnp
from jax import lax

D = 1536
HEADS = 24
HEAD_DIM = 64
FF = 4096
TDIM = 4096
CDIM = 1024
TEXT = 256
GRID = 48
LEN = 2352
ITEMS_ALL = 4


def draw_caption_len(key, part):
    lengths = jax.random.randint(key, (ITEMS_ALL,), 1, TEXT + 1)
    chosen = jax.random.randint(jax.random.fold_in(key, 7), (), 0, ITEMS_ALL)
    return lengths.at[chosen].set(TEXT).astype(jnp.int32)


def draw_image_shape(key, part):
    widths = jax.random.randint(jax.random.fold_in(key, 1), (ITEMS_ALL,), GRID // 4, GRID + 1)
    heights = jax.random.randint(jax.random.fold_in(key, 2), (ITEMS_ALL,), GRID // 2, GRID + 1)
    chosen = jax.random.randint(jax.random.fold_in(key, 3), (), 0, ITEMS_ALL)
    heights = heights.at[chosen].set(GRID)
    widths = widths.at[chosen].set(GRID)
    return jnp.stack([heights, widths], axis=1).astype(jnp.int32)


def shard_levels(rng, dims, cuts, least, top_value):
    def one(dim, blocks):
        steps = jax.random.uniform(jax.random.fold_in(jax.random.fold_in(rng, 6), dim), (blocks,), jnp.float32, least / len(cuts), top_value / len(cuts))
        return jnp.repeat(jnp.exp(steps), dims[dim] // blocks).reshape((-1,) + (1,) * (len(dims) - dim - 1))

    level = one(*cuts[0])
    for cut in cuts[1:]:
        level = level * one(*cut)
    return level


def centred(key, extent, scale, bound, cuts=(), dtype=jnp.bfloat16):
    factor_of = shard_levels(key, extent, cuts, -0.22, 0.18) if cuts else 1.0
    array = jax.random.normal(key, extent, jnp.float32) * scale * factor_of
    return jnp.minimum(jnp.maximum(array, -bound), bound).astype(dtype)


def setup_inputs(seed: int = 0) -> dict:
    streams_of = jax.random.split(jax.random.key(seed), 16)
    return {
        "tokens": centred(streams_of[0], (ITEMS_ALL, LEN, D), 1.0, 6.0, ((0, 4), (1, 8))),
        "condition": centred(streams_of[1], (ITEMS_ALL, CDIM), 1.0, 6.0, ((1, 32),), jnp.float32),
        "caption": centred(streams_of[2], (ITEMS_ALL, TEXT, TDIM), 1.0, 6.0, ((2, 32),)),
        "caption_len": draw_caption_len(jax.random.fold_in(streams_of[15], 71), 0),
        "image_shape": draw_image_shape(jax.random.fold_in(streams_of[15], 71), 0),
        "cotangent": centred(streams_of[5], (ITEMS_ALL, LEN, D), 1.0, 6.0, ((0, 4), (1, 8))),
        "joint_weight": centred(streams_of[6], (D, 3 * D), D ** -0.5, 0.15625, ((0, 32),)),
        "mixer_weight": centred(streams_of[7], (D, D), D ** -0.5, 0.15625, ((0, 32),)),
        "gate_up_weight": centred(streams_of[8], (D, 2 * FF), D ** -0.5, 0.15625, ((0, 32),)),
        "down_weight": centred(streams_of[9], (FF, D), FF ** -0.5, 0.09375, ((0, 32),)),
        "text_weight": centred(streams_of[10], (TDIM, 2 * D), TDIM ** -0.5, 0.09375, ((0, 32),)),
        "modulation_weight": centred(streams_of[11], (CDIM, 6 * D), CDIM ** -0.5, 0.1875, ((0, 32),)),
        "modulation_bias": centred(streams_of[12], (6 * D,), 0.5, 3.0, ((0, 32),), jnp.float32),
        "norm_gains": jnp.clip(1.0 + 0.15 * jax.random.normal(streams_of[13], (7, D), jnp.float32), 0.25, 1.75).astype(jnp.bfloat16),
        "head_gates": jnp.clip(jax.random.uniform(streams_of[14], (HEADS,), jnp.float32, -1.5, 1.5), -1.5, 1.5),
    }


EPS = 1e-06
HIGH = lax.Precision.HIGHEST

@jax.custom_vjp
def low(v):
    return lax.optimization_barrier(v.astype(jnp.bfloat16)).astype(jnp.float32)

@jax.custom_vjp
def low_back(v):
    return v

def low_keep(v):
    return (low(v), None)

def low_pass(kept, grad):
    return (grad,)

def back_keep(v):
    return (v, None)

def back_low(kept, grad):
    return (low(grad),)
low.defvjp(low_keep, low_pass)
low_back.defvjp(back_keep, back_low)

def norm_rows(v, gain):
    return v * lax.rsqrt(lax.optimization_barrier(jnp.mean(v * v, axis=-1, keepdims=True)) + EPS) * gain

def rotate(v, positions):
    half = HEAD_DIM // 2
    freq = jnp.exp(jnp.arange(half).astype(jnp.float32) * (-jnp.log(10000.0) / half))
    angle = positions.astype(jnp.float32)[:, None] * freq[None, :]
    cosine = jnp.cos(angle)[:, None, :]
    sine = jnp.sin(angle)[:, None, :]
    heads = v.reshape(v.shape[0], HEADS, HEAD_DIM)
    first = heads[..., :half]
    second = heads[..., half:]
    turned = jnp.concatenate([first * cosine - second * sine, first * sine + second * cosine], axis=-1)
    return turned.reshape(v.shape[0], HEADS * HEAD_DIM)

def attend(queries, keys, values, valid):
    scale = float(HEAD_DIM) ** (-0.5)
    query_heads = queries.reshape(queries.shape[0], HEADS, HEAD_DIM)
    key_heads = keys.reshape(keys.shape[0], HEADS, HEAD_DIM)
    value_heads = values.reshape(values.shape[0], HEADS, HEAD_DIM)
    raw = jnp.einsum('qhd,khd->hqk', query_heads, key_heads, precision=HIGH)
    scores = low_back(raw) * scale
    live = jnp.arange(keys.shape[0]) < valid
    scores = jnp.where(live[None, None, :], scores, -1e+30)
    probs = low(jax.nn.softmax(scores, axis=-1))
    mixed = jnp.einsum('hqk,khd->qhd', probs, value_heads, precision=HIGH)
    return mixed.reshape(queries.shape[0], HEADS * HEAD_DIM)

def item_layer(x, text, mod, length, shape, joint_w, mixer_w, gate_up_w, down_w, text_w, gains, gates):
    shift_a = mod[0:D]
    scale_a = mod[D:2 * D]
    gate_a = mod[2 * D:3 * D]
    shift_f = mod[3 * D:4 * D]
    scale_f = mod[4 * D:5 * D]
    gate_f = mod[5 * D:6 * D]
    normed_in = low(norm_rows(x, gains[0]) * (1.0 + scale_a) + shift_a)
    joint = low_back(jnp.dot(normed_in, joint_w, precision=HIGH))
    positions = jnp.arange(LEN)
    queries = low(rotate(norm_rows(joint[:, :D], gains[4]), positions))
    keys = low(rotate(norm_rows(joint[:, D:2 * D], gains[5]), positions))
    values = low(joint[:, 2 * D:])
    text_raw = low_back(jnp.dot(low(text), text_w, precision=HIGH))
    text_keys = low(norm_rows(text_raw[:, :D], gains[6]))
    text_values = low(text_raw[:, D:])
    valid = shape[0] * (shape[1] + 1)
    gate_cols = jnp.repeat(jnp.tanh(gates), HEAD_DIM)
    block = LEN // 8

    def one_block(start):
        rows = lax.dynamic_slice_in_dim(queries, start, block, 0)
        own = attend(rows, keys, values, valid)
        cross = low_back(attend(rows, text_keys, text_values, length))
        return own + gate_cols * cross
    starts = (jnp.arange(8) * block).astype(jnp.int32)
    mixed = lax.map(jax.checkpoint(one_block), starts).reshape(LEN, D)
    mixed = low_back(low(mixed))
    proj = low_back(jnp.dot(mixed, mixer_w, precision=HIGH))
    h = x + gate_a * norm_rows(proj, gains[1])
    ffn_in = low(norm_rows(h, gains[2]) * (1.0 + scale_f) + shift_f)
    gate_up = low_back(jnp.dot(ffn_in, gate_up_w, precision=HIGH))
    hidden = low(jax.nn.silu(gate_up[:, :FF]) * gate_up[:, FF:])
    ffn = low_back(jnp.dot(hidden, down_w, precision=HIGH))
    return h + gate_f * norm_rows(ffn, gains[3])

def reference(tokens, condition, caption, caption_len, image_shape, cotangent, joint_weight, mixer_weight, gate_up_weight, down_weight, text_weight, modulation_weight, modulation_bias, norm_gains, head_gates):
    caption_f = caption.astype(jnp.float32)
    soft_cond = low(jax.nn.silu(condition.astype(jnp.float32)))
    run_item = jax.checkpoint(item_layer)

    def layer(x, joint_w, mixer_w, gate_up_w, down_w, text_w, mod_w, mod_b, gains, gates):
        mods = low_back(jnp.dot(soft_cond, mod_w, precision=HIGH) + mod_b)

        def step(carry, parts):
            x_item, text_item, mod_item, length, shape = parts
            result = run_item(x_item, text_item, mod_item, length, shape, joint_w, mixer_w, gate_up_w, down_w, text_w, gains, gates)
            return (carry, result)
        _, outs = lax.scan(step, jnp.zeros((), jnp.float32), (x, caption_f, mods, caption_len, image_shape))
        return outs
    primals = (tokens.astype(jnp.float32), joint_weight.astype(jnp.float32), mixer_weight.astype(jnp.float32), gate_up_weight.astype(jnp.float32), down_weight.astype(jnp.float32), text_weight.astype(jnp.float32), modulation_weight.astype(jnp.float32), modulation_bias.astype(jnp.float32), norm_gains.astype(jnp.float32), head_gates.astype(jnp.float32))
    output, pull = jax.vjp(layer, *primals)
    grads = pull(cotangent.astype(jnp.float32))
    return (output.astype(jnp.bfloat16), grads[0].astype(jnp.bfloat16), grads[1], grads[2], grads[3], grads[4], grads[5], grads[6], grads[7], grads[8], grads[9])
```

```python
import functools

import jax
import jax.numpy as jnp
from jax import lax
from jax.experimental import pallas as pl
from jax.experimental.pallas import tpu as pltpu
from jax.sharding import Mesh
from jax.sharding import PartitionSpec as P

HEADS = 24
HEAD_DIM = 64
TEXT = 256
WIDTH = HEADS * HEAD_DIM
EPS = 1e-06
NEG = -1e30
SCALE = float(HEAD_DIM) ** (-0.5)
LANES = 128
BF = jnp.bfloat16
F32 = jnp.float32
VMEM_BYTES = 56 << 20


def norm_rows(v, gain):
    return v * lax.rsqrt(jnp.mean(v * v, axis=-1, keepdims=True) + EPS) * gain


def modulate(v, gain, scale, shift):
    return norm_rows(v, gain) * (1.0 + scale) + shift


def branch_out(v, gain, gate):
    return gate * norm_rows(v, gain)


def swiglu(gate_up):
    half = gate_up.shape[-1] // 2
    return jax.nn.silu(gate_up[:, :half]) * gate_up[:, half:]


def product(left, right):
    return jnp.dot(left, right, preferred_element_type=F32)


def contract(left, right, left_dim, right_dim):
    return lax.dot_general(
        left, right, (((left_dim,), (right_dim,)), ((), ())), preferred_element_type=F32
    )


def split3(v):
    high = v.astype(BF)
    rest = v - high.astype(F32)
    mid = rest.astype(BF)
    return [high, mid, (rest - mid.astype(F32)).astype(BF)]


def extend(block, columns):
    rows = block.shape[0]
    fill = HEAD_DIM - len(columns)
    return jnp.concatenate([block] + list(columns) + [jnp.zeros((rows, fill), BF)], axis=1)


def spread_keys(heads, qkv_ref, text_ref, bias_ref, text_bias_ref, outs, key_ones, value_ones):
    wide = heads * HEAD_DIM
    for source, bias, key_out, value_out, start in (
        (qkv_ref, bias_ref, outs[0], outs[1], wide),
        (text_ref, text_bias_ref, outs[2], outs[3], 0),
    ):
        one = jnp.ones((source.shape[0], 1), BF)
        for h in range(heads):
            at = start + h * HEAD_DIM
            key_out[h] = extend(source[:, at : at + HEAD_DIM], [bias[...]] + [one] * key_ones)
            at = at + wide
            value_out[h] = extend(source[:, at : at + HEAD_DIM], [one] * value_ones)


def attend_forward_kernel(
    heads, qkv_ref, text_ref, bias_ref, text_bias_ref, gate_ref, q_ref,
    mixed_ref, own_ref, cross_ref, lse_ref, *spread
):
    @pl.when(pl.program_id(0) == 0)
    def _():
        spread_keys(heads, qkv_ref, text_ref, bias_ref, text_bias_ref, spread, 0, 1)

    one = jnp.ones((q_ref.shape[0], 1), BF)

    def soft(query, keys, values):
        scores = contract(query, keys[...], 1, 1)
        high = jnp.max(scores, axis=1, keepdims=True)
        total = contract(jnp.exp(scores - high).astype(BF), values[...], 1, 0)
        mass = total[:, HEAD_DIM : HEAD_DIM + 1]
        return total[:, :HEAD_DIM] / mass, high + jnp.log(mass)

    own, cross, lse = [], [], []
    for h in range(heads):
        at = h * HEAD_DIM
        query = extend(q_ref[:, at : at + HEAD_DIM] * SCALE, [one])
        mixed, own_lse = soft(query, spread[0].at[h], spread[1].at[h])
        own.append(mixed)
        mixed, cross_lse = soft(query, spread[2].at[h], spread[3].at[h])
        cross.append(mixed)
        lse += [own_lse, cross_lse]
    own = jnp.concatenate(own, axis=1)
    cross = jnp.concatenate(cross, axis=1)
    own_ref[...] = own
    cross_ref[...] = cross
    mixed_ref[...] = (own + gate_ref[...] * cross).astype(BF)
    lse_ref[...] = jnp.concatenate(lse, axis=1)


def attend_backward_kernel(
    heads, qkv_ref, text_ref, bias_ref, text_bias_ref, gate_ref, q_ref, up_ref, own_ref, cross_ref, lse_ref,
    dq_ref, dkv_ref, dtext_ref, dgate_ref, *scratch
):
    spread, sums = scratch[:4], scratch[4:]
    step = pl.program_id(0)

    @pl.when(step == 0)
    def _():
        spread_keys(heads, qkv_ref, text_ref, bias_ref, text_bias_ref, spread, 3, 3)
        for ref in sums + (dgate_ref,):
            ref[...] = jnp.zeros_like(ref)

    one = jnp.ones((q_ref.shape[0], 1), BF)
    up = up_ref[...]
    up_float = up.astype(F32)
    up_cross = (gate_ref[...] * up_float).astype(BF)
    dgate_ref[...] += jnp.sum(up_float * cross_ref[...], axis=0, keepdims=True)
    own_row = up_float * own_ref[...]
    cross_row = up_cross.astype(F32) * cross_ref[...]
    dq = []
    for h in range(heads):
        cut = slice(h * HEAD_DIM, (h + 1) * HEAD_DIM)
        query = q_ref[:, cut]
        scaled = query * SCALE

        def one_soft(upstream, row, lse, keys, values, key_sum, value_sum):
            center = jnp.sum(row, axis=1, keepdims=True)
            left = extend(scaled, [one] + [-part for part in split3(lse)])
            weights = jnp.exp(contract(left, keys[...], 1, 1))
            left = extend(upstream, [-part for part in split3(center)])
            score_grad = (weights * contract(left, values[...], 1, 1)).astype(BF)
            weights = weights.astype(BF)
            key_sum[...] += contract(score_grad, query, 0, 0)
            value_sum[...] += contract(weights, upstream, 0, 0)
            return contract(score_grad, keys[...], 1, 0)[:, :HEAD_DIM]

        part = one_soft(
            up[:, cut], own_row[:, cut], lse_ref[:, 2 * h : 2 * h + 1],
            spread[0].at[h], spread[1].at[h], sums[0].at[h], sums[1].at[h],
        )
        part += one_soft(
            up_cross[:, cut], cross_row[:, cut], lse_ref[:, 2 * h + 1 : 2 * h + 2],
            spread[2].at[h], spread[3].at[h], sums[2].at[h], sums[3].at[h],
        )
        dq.append(part * SCALE)
    dq_ref[...] = jnp.concatenate(dq, axis=1).astype(BF)

    @pl.when(step == pl.num_programs(0) - 1)
    def _():
        for out, key_sum, value_sum in ((dkv_ref, sums[0], sums[1]), (dtext_ref, sums[2], sums[3])):
            parts = [key_sum[h] * SCALE for h in range(heads)] + [value_sum[h] for h in range(heads)]
            out[...] = jnp.concatenate(parts, axis=1).astype(BF)


def whole_block(shape):
    return pl.BlockSpec(shape, lambda i: (0,) * len(shape), pipeline_mode=pl.Buffered(1))


def row_block(rows, columns):
    return pl.BlockSpec((rows, columns), lambda i: (i, 0))


def spread_scratch(heads, slots, text):
    return [pltpu.VMEM((heads, n, 2 * HEAD_DIM), BF) for n in (slots, slots, text, text)]


def attend_forward(qkv, text, bias, text_bias, gate, heads, rows):
    slots, wide, words = qkv.shape[0], heads * HEAD_DIM, text.shape[0]
    return pl.pallas_call(
        functools.partial(attend_forward_kernel, heads),
        grid=(slots // rows,),
        in_specs=[
            whole_block((slots, 3 * wide)), whole_block((words, 2 * wide)), whole_block((slots, 1)),
            whole_block((words, 1)), whole_block((1, wide)), row_block(rows, wide),
        ],
        out_specs=[row_block(rows, wide)] * 3 + [row_block(rows, 2 * heads)],
        out_shape=[
            jax.ShapeDtypeStruct((slots, wide), BF),
            jax.ShapeDtypeStruct((slots, wide), F32),
            jax.ShapeDtypeStruct((slots, wide), F32),
            jax.ShapeDtypeStruct((slots, 2 * heads), F32),
        ],
        scratch_shapes=spread_scratch(heads, slots, words),
        compiler_params=pltpu.CompilerParams(vmem_limit_bytes=VMEM_BYTES),
        cost_estimate=pl.CostEstimate(
            flops=16 * slots * (slots + words) * wide,
            bytes_accessed=slots * wide * 18,
            transcendentals=slots * (slots + words) * heads,
        ),
        name="attend_forward",
    )(qkv, text, bias, text_bias, gate, qkv[:, :wide])


def attend_backward(qkv, text, bias, text_bias, gate, up, own, cross, lse, heads, rows):
    slots, wide, words = qkv.shape[0], heads * HEAD_DIM, text.shape[0]
    return pl.pallas_call(
        functools.partial(attend_backward_kernel, heads),
        grid=(slots // rows,),
        in_specs=[
            whole_block((slots, 3 * wide)), whole_block((words, 2 * wide)), whole_block((slots, 1)),
            whole_block((words, 1)), whole_block((1, wide)),
            row_block(rows, wide), row_block(rows, wide), row_block(rows, wide), row_block(rows, wide),
            row_block(rows, 2 * heads),
        ],
        out_specs=[
            row_block(rows, wide), whole_block((slots, 2 * wide)), whole_block((words, 2 * wide)),
            whole_block((1, wide)),
        ],
        out_shape=[
            jax.ShapeDtypeStruct((slots, wide), BF),
            jax.ShapeDtypeStruct((slots, 2 * wide), BF),
            jax.ShapeDtypeStruct((words, 2 * wide), BF),
            jax.ShapeDtypeStruct((1, wide), F32),
        ],
        scratch_shapes=spread_scratch(heads, slots, words)
        + [pltpu.VMEM((heads, n, HEAD_DIM), F32) for n in (slots, slots, words, words)],
        compiler_params=pltpu.CompilerParams(vmem_limit_bytes=VMEM_BYTES),
        cost_estimate=pl.CostEstimate(
            flops=40 * slots * (slots + words) * wide,
            bytes_accessed=slots * wide * 26,
            transcendentals=slots * (slots + words) * heads,
        ),
        name="attend_backward",
    )(qkv, text, bias, text_bias, gate, qkv[:, :wide], up, own, cross, lse)


def swap_halves(v):
    lane = lax.broadcasted_iota(jnp.int32, v.shape, 1)
    half = HEAD_DIM // 2
    return jnp.where(
        lane % HEAD_DIM < half, pltpu.roll(v, LANES - half, 1), pltpu.roll(v, half, 1)
    )


def tiles_of(v):
    return [v[:, t : t + LANES] for t in range(0, v.shape[1], LANES)]


def group_kernel(heads, groups, joint_ref, gains_ref, cos_ref, sin_ref, out_ref):
    wide = heads * HEAD_DIM
    cosine, sine = cos_ref[...], sin_ref[...]
    parts = []
    for which in range(2):
        raw = joint_ref[:, which * WIDTH : (which + 1) * WIDTH]
        root = lax.rsqrt(jnp.mean(raw * raw, axis=1, keepdims=True) + EPS)
        scaled = raw * root * gains_ref[which : which + 1, :]
        turned = [tile * cosine + swap_halves(tile) * sine for tile in tiles_of(scaled)]
        parts.append(jnp.concatenate(turned, axis=1).astype(BF))
    parts.append(joint_ref[:, 2 * WIDTH :].astype(BF))
    for g in range(groups):
        for which, part in enumerate(parts):
            at = g * wide
            size = max(0, min(wide, WIDTH - at))
            if size:
                out_ref[g, :, which * wide : which * wide + size] = part[:, at : at + size]
            if size < wide:
                out_ref[g, :, which * wide + size : (which + 1) * wide] = jnp.zeros(
                    (part.shape[0], wide - size), BF
                )


def ungroup_kernel(heads, groups, grad_ref, joint_ref, gains_ref, cos_ref, sin_ref, out_ref, dgain_ref):
    wide = heads * HEAD_DIM
    cosine, sine = cos_ref[...], sin_ref[...]

    @pl.when(pl.program_id(0) == 0)
    def _():
        dgain_ref[...] = jnp.zeros_like(dgain_ref)

    def rows_of(which):
        parts = []
        for g in range(groups):
            size = max(0, min(wide, WIDTH - g * wide))
            if size:
                parts.append(grad_ref[g, :, which * wide : which * wide + size])
        return jnp.concatenate(parts, axis=1)

    for which in range(2):
        cut = slice(which * WIDTH, (which + 1) * WIDTH)
        grad = rows_of(which).astype(F32)
        turned = [tile * cosine - swap_halves(tile) * sine for tile in tiles_of(grad)]
        grad = jnp.concatenate(turned, axis=1)
        raw = joint_ref[:, cut]
        root = lax.rsqrt(jnp.mean(raw * raw, axis=1, keepdims=True) + EPS)
        unit = raw * root
        dgain_ref[which : which + 1, :] += jnp.sum(grad * unit, axis=0, keepdims=True)
        grad = grad * gains_ref[which : which + 1, :]
        grad = root * (grad - unit * jnp.mean(grad * unit, axis=1, keepdims=True))
        out_ref[:, cut] = grad.astype(BF)
    out_ref[:, 2 * WIDTH :] = rows_of(2)


def group_heads(joint, gains, cosine, sine, heads, groups):
    rows = joint.shape[0]
    block = rows // 2
    return pl.pallas_call(
        functools.partial(group_kernel, heads, groups),
        grid=(2,),
        in_specs=[
            row_block(block, 3 * WIDTH), whole_block((2, WIDTH)), row_block(block, LANES), row_block(block, LANES)
        ],
        out_specs=pl.BlockSpec((groups, block, 3 * heads * HEAD_DIM), lambda i: (0, i, 0)),
        out_shape=jax.ShapeDtypeStruct((groups, rows, 3 * heads * HEAD_DIM), BF),
        compiler_params=pltpu.CompilerParams(vmem_limit_bytes=VMEM_BYTES),
        cost_estimate=pl.CostEstimate(
            flops=rows * WIDTH * 30, bytes_accessed=rows * WIDTH * 18, transcendentals=rows
        ),
        name="group_heads",
    )(joint, gains, cosine, sine)


def ungroup_heads(grads, joint, gains, cosine, sine, heads):
    groups, rows, wide = grads.shape
    block = rows // 2
    return pl.pallas_call(
        functools.partial(ungroup_kernel, heads, groups),
        grid=(2,),
        in_specs=[
            pl.BlockSpec((groups, block, wide), lambda i: (0, i, 0)),
            row_block(block, 3 * WIDTH), whole_block((2, WIDTH)), row_block(block, LANES), row_block(block, LANES),
        ],
        out_specs=[row_block(block, 3 * WIDTH), whole_block((2, WIDTH))],
        out_shape=[
            jax.ShapeDtypeStruct((rows, 3 * WIDTH), BF),
            jax.ShapeDtypeStruct((2, WIDTH), F32),
        ],
        compiler_params=pltpu.CompilerParams(vmem_limit_bytes=VMEM_BYTES),
        cost_estimate=pl.CostEstimate(
            flops=rows * WIDTH * 50, bytes_accessed=rows * WIDTH * 24, transcendentals=rows
        ),
        name="ungroup_heads",
    )(grads, joint, gains, cosine, sine)


def local(
    sizes,
    tokens,
    condition,
    caption,
    caption_len,
    image_shape,
    cotangent,
    joint_weight,
    mixer_weight,
    gate_up_weight,
    down_weight,
    text_weight,
    modulation_weight,
    modulation_bias,
    norm_gains,
    head_gates,
):
    n_dp, n_z, n_core = sizes
    everyone = ("dp", "z", "core")
    seq = ("z", "core")
    n_seq = n_z * n_core
    heads = -(-HEADS // n_seq)
    wide = heads * HEAD_DIM
    spare = n_seq * heads - HEADS
    rows = tokens.shape[1]
    slots = -(-rows // 16) * 16
    dp = lax.axis_index("dp")
    core = lax.axis_index("core")
    seq_index = lax.axis_index(seq)
    device = lax.axis_index(everyone)

    def swap(v, axis, n, k):
        return lax.ppermute(v, axis, [(i, i ^ k) for i in range(n)])

    def tree(parts):
        while len(parts) > 1:
            parts = [parts[i] + parts[i + 1] for i in range(0, len(parts), 2)]
        return parts[0]

    def sum_over(v, axis, n):
        return tree([v] + [swap(v, axis, n, k) for k in range(1, n)])

    soft_cond = jax.nn.silu(condition).astype(BF)
    partial_mods = product(soft_cond, modulation_weight)
    bias_width = modulation_bias.shape[0]
    bias_start = device * bias_width
    with_bias = (
        lax.dynamic_slice_in_dim(partial_mods, bias_start, bias_width, 1) + modulation_bias[None, :]
    )
    partial_mods = lax.dynamic_update_slice_in_dim(partial_mods, with_bias, bias_start, 1)
    mods_width = partial_mods.shape[1]
    gain_rows, gain_width = norm_gains.shape
    own_gains = lax.dynamic_update_slice_in_dim(
        jnp.zeros((gain_rows, WIDTH), F32), norm_gains.astype(F32), device * gain_width, 1
    ).reshape(1, -1)

    def message(item):
        return jnp.concatenate([lax.dynamic_slice_in_dim(partial_mods, item, 1, 0), own_gains], axis=1)

    head_vector = tree(
        [message(dp)] + [swap(message(dp ^ k), "dp", n_dp, k) for k in range(1, n_dp)]
    )
    head_vector = sum_over(sum_over(head_vector, "core", n_core), "z", n_z)
    mods = head_vector[:, :mods_width]
    gains = head_vector[0, mods_width:].reshape(gain_rows, WIDTH)
    shift_a, scale_a, gate_a, shift_f, scale_f, gate_f = [
        jnp.broadcast_to(mods[:, i * WIDTH : (i + 1) * WIDTH], (slots, WIDTH)) for i in range(6)
    ]

    joint_full, mixer_full, gate_up_full, down_full = (
        lax.all_gather(joint_weight, everyone, axis=0, tiled=True),
        lax.all_gather(mixer_weight, everyone, axis=0, tiled=True),
        lax.all_gather(gate_up_weight, everyone, axis=0, tiled=True),
        lax.all_gather(down_weight, everyone, axis=0, tiled=True),
    )

    flat_text = caption.reshape(-1, caption.shape[2])
    text_raw = lax.psum_scatter(
        product(flat_text, text_weight).astype(BF), everyone, scatter_dimension=0, tiled=True
    ).astype(F32)
    text_rows = text_raw.shape[0]
    text_keys, text_key_pull = jax.vjp(norm_rows, text_raw[:, :WIDTH], gains[6])

    def to_groups(parts):
        count = parts[0].shape[0]
        spread = []
        for part in parts:
            part = jnp.pad(part, ((0, 0), (0, spare * HEAD_DIM)))
            spread.append(part.reshape(count, n_seq, wide).transpose(1, 0, 2))
        return jnp.concatenate(spread, axis=2)

    def from_groups(grouped, which):
        part = grouped[:, :, which * wide : (which + 1) * wide].transpose(1, 0, 2)
        return part.reshape(part.shape[0], n_seq * wide)[:, :WIDTH]

    def exchange(v):
        return lax.all_to_all(v, seq, 0, 0, tiled=True)

    text_own = exchange(
        to_groups([text_keys.astype(BF), text_raw[:, WIDTH:].astype(BF)])
    ).reshape(n_seq * text_rows, 2 * wide)

    pad = ((0, slots - rows), (0, 0))
    xfloat = jnp.pad(tokens[0], pad).astype(F32)
    upstream = jnp.pad(cotangent[0], pad).astype(F32)
    normed_in, normed_pull = jax.vjp(modulate, xfloat, gains[0], scale_a, shift_a)
    normed_low = normed_in.astype(BF)
    joint = product(normed_low, joint_full)
    lane = jnp.arange(LANES)
    freq = jnp.exp((lane % (HEAD_DIM // 2)).astype(F32) * (-jnp.log(10000.0) / (HEAD_DIM // 2)))
    angle = (seq_index * rows + jnp.arange(slots)).astype(F32)[:, None] * freq[None, :]
    cosine = jnp.cos(angle)
    sine = jnp.sin(angle) * jnp.where(lane % HEAD_DIM < HEAD_DIM // 2, -1.0, 1.0)[None, :]
    rope_gains = gains[4:6]
    qkv = exchange(group_heads(joint, rope_gains, cosine, sine, heads, n_seq)).reshape(
        n_seq * slots, 3 * wide
    )
    place = jnp.arange(n_seq * slots)
    within = place % slots
    shape_row = image_shape[dp]
    valid = shape_row[0] * (shape_row[1] + 1)
    live = (within < rows) & ((place // slots) * rows + within < valid)
    bias = jnp.where(live, 0.0, NEG).astype(BF)[:, None]
    text_bias = jnp.where(jnp.arange(TEXT) < caption_len[dp], 0.0, NEG).astype(BF)[:, None]
    tanh_gates = jnp.tanh(head_gates)
    first_head = seq_index * heads
    own_gates = lax.dynamic_slice_in_dim(jnp.pad(tanh_gates, (0, spare)), first_head, heads, 0)
    gate_row = jnp.repeat(own_gates, HEAD_DIM)[None, :]
    attend_args = (qkv, text_own, bias, text_bias, gate_row)
    mixed_own, own_out, cross_out, lse = attend_forward(*attend_args, heads, 2 * slots)
    mixed = from_groups(exchange(mixed_own.reshape(n_seq, slots, wide)), 0)
    proj = product(mixed, mixer_full)
    branch_a, branch_a_pull = jax.vjp(branch_out, proj, gains[1], gate_a)
    hstate = xfloat + branch_a
    ffn_in, ffn_in_pull = jax.vjp(modulate, hstate, gains[2], scale_f, shift_f)
    ffn_low = ffn_in.astype(BF)
    gate_up = product(ffn_low, gate_up_full)
    hidden, swiglu_pull = jax.vjp(swiglu, gate_up)
    hidden_low = hidden.astype(BF)
    ffn = product(hidden_low, down_full)
    branch_f, branch_f_pull = jax.vjp(branch_out, ffn, gains[3], gate_f)
    output = (hstate + branch_f).astype(BF)[None, :rows]

    def weight_grad(left, right):
        half = right.shape[1] // n_core
        both_left = jnp.concatenate([left, swap(left, "core", n_core, 1)], axis=0)
        mine = lax.dynamic_slice_in_dim(right, core * half, half, 1)
        other = lax.dynamic_slice_in_dim(right, (1 - core) * half, half, 1)
        both_right = jnp.concatenate([mine, swap(other, "core", n_core, 1)], axis=0)
        part = contract(both_left, both_right, 0, 0).astype(BF)
        part = lax.psum_scatter(part, ("dp", "z"), scatter_dimension=0, tiled=True)
        count = part.shape[0] // n_core
        kept = lax.dynamic_slice_in_dim(part, core * count, count, 0)
        sent = lax.dynamic_slice_in_dim(part, (1 - core) * count, count, 0)
        received = swap(sent, "core", n_core, 1)
        first = jnp.where(core == 0, kept, received)
        second = jnp.where(core == 0, received, kept)
        return jnp.concatenate([first, second], axis=1).astype(F32)

    ffn_grad, gain3_grad, gate_f_grad = branch_f_pull(upstream)
    ffn_grad_low = ffn_grad.astype(BF)
    down_out = weight_grad(hidden_low, ffn_grad_low)
    (gate_up_grad_rows,) = swiglu_pull(contract(ffn_grad_low, down_full, 1, 1))
    gate_up_low = gate_up_grad_rows.astype(BF)
    gate_up_out = weight_grad(ffn_low, gate_up_low)
    state_part, gain2_grad, scale_f_grad, shift_f_grad = ffn_in_pull(
        contract(gate_up_low, gate_up_full, 1, 1)
    )
    state_grad = upstream + state_part
    proj_grad, gain1_grad, gate_a_grad = branch_a_pull(state_grad)
    proj_low = proj_grad.astype(BF)
    mixer_out = weight_grad(mixed, proj_low)
    mixed_grad = contract(proj_low, mixer_full, 1, 1).astype(BF)
    up_own = exchange(to_groups([mixed_grad])).reshape(n_seq * slots, wide)
    dq, dkv, dtext, dgate = attend_backward(
        *attend_args, up_own, own_out, cross_out, lse, heads, 2 * slots
    )
    grouped = exchange(jnp.concatenate([dq, dkv], axis=1).reshape(n_seq, slots, 3 * wide))
    joint_low, rope_gain_grads = ungroup_heads(grouped, joint, rope_gains, cosine, sine, heads)
    joint_out = weight_grad(normed_low, joint_low)
    input_part, gain0_grad, scale_a_grad, shift_a_grad = normed_pull(
        contract(joint_low, joint_full, 1, 1)
    )
    tokens_grad = (state_grad + input_part).astype(BF)[None, :rows]
    text_back = exchange(dtext.reshape(n_seq, text_rows, 2 * wide))
    text_key_grad, gain6_grad = text_key_pull(from_groups(text_back, 0).astype(F32))
    text_grad_rows = jnp.concatenate([text_key_grad.astype(BF), from_groups(text_back, 1)], axis=1)
    text_grad_all = lax.all_gather(text_grad_rows, everyone, axis=0, tiled=True)
    text_grad = contract(flat_text, text_grad_all, 0, 0)

    gates_own = jnp.sum(dgate.reshape(heads, HEAD_DIM), axis=1) * (1.0 - own_gates * own_gates)
    gates_all = lax.dynamic_update_slice_in_dim(
        jnp.zeros((HEADS + spare,), F32), gates_own, first_head, 0
    )
    pieces = [
        jnp.sum(value, axis=0)
        for value in (shift_a_grad, scale_a_grad, gate_a_grad, shift_f_grad, scale_f_grad, gate_f_grad)
    ]
    shared = [gain0_grad, gain1_grad, gain2_grad, gain3_grad, rope_gain_grads[0], rope_gain_grads[1], gain6_grad]
    tail = jnp.concatenate(pieces + shared + [gates_all])
    tail = sum_over(sum_over(tail, "core", n_core), "z", n_z)
    tails = [tail] + [swap(tail, "dp", n_dp, k) for k in range(1, n_dp)]
    total = tree([t[mods_width:] for t in tails])
    gates_grad = total[gain_rows * WIDTH : gain_rows * WIDTH + HEADS]
    gains_grad = lax.dynamic_slice_in_dim(
        total[: gain_rows * WIDTH].reshape(gain_rows, WIDTH), device * gain_width, gain_width, 1
    )
    mods_low = jnp.stack([t[:mods_width].astype(BF) for t in tails])
    cond_rows = jnp.concatenate(
        [lax.dynamic_slice_in_dim(soft_cond, dp ^ k, 1, 0) for k in range(n_dp)], axis=0
    )
    modulation_grad = contract(cond_rows, mods_low, 0, 0)
    bias_grad = lax.dynamic_slice_in_dim(
        jnp.sum(mods_low.astype(F32), axis=0), bias_start, bias_width, 0
    )
    return (
        output,
        tokens_grad,
        joint_out,
        mixer_out,
        gate_up_out,
        down_out,
        text_grad,
        modulation_grad,
        bias_grad,
        gains_grad,
        gates_grad,
    )


def solution(mesh):
    n_dp, n_seq = mesh.shape["dp"], mesh.shape["seq"]
    sizes = (n_dp, n_seq // 2, 2)
    split = Mesh(mesh.devices.reshape(sizes), ("dp", "z", "core"))
    seq, everyone = ("z", "core"), ("dp", "z", "core")
    token_spec, row_spec, column_spec = P("dp", seq, None), P(everyone, None), P(None, everyone)
    in_specs = (
        token_spec, column_spec, P(None, None, everyone), P(), P(), token_spec,
        row_spec, row_spec, row_spec, row_spec, row_spec, row_spec, P(everyone), column_spec, P(),
    )
    out_specs = (
        token_spec, token_spec, row_spec, row_spec, row_spec, row_spec, row_spec, row_spec,
        P(everyone), column_spec, P(),
    )
    return jax.shard_map(
        functools.partial(local, sizes), mesh=split, in_specs=in_specs, out_specs=out_specs, check_vma=False
    )
```

```python
import functools

import jax
import jax.numpy as jnp
from jax import lax
from jax.experimental import pallas as pl
from jax.experimental.pallas import tpu as pltpu
from jax.sharding import Mesh
from jax.sharding import PartitionSpec as P

HEADS = 24
HEAD_DIM = 64
TEXT = 256
WIDTH = HEADS * HEAD_DIM
EPS = 1e-06
NEG = -1e30
SCALE = float(HEAD_DIM) ** (-0.5)
LANES = 128
BF = jnp.bfloat16
F32 = jnp.float32
VMEM_BYTES = 56 << 20


def norm_rows(v, gain):
    return v * lax.rsqrt(jnp.mean(v * v, axis=-1, keepdims=True) + EPS) * gain


def modulate(v, gain, scale, shift):
    return norm_rows(v, gain) * (1.0 + scale) + shift


def branch_out(v, gain, gate):
    return gate * norm_rows(v, gain)


def swiglu(gate_up):
    half = gate_up.shape[-1] // 2
    return jax.nn.silu(gate_up[:, :half]) * gate_up[:, half:]


def product(left, right):
    return jnp.dot(left, right, preferred_element_type=F32)


def contract(left, right, left_dim, right_dim):
    return lax.dot_general(
        left, right, (((left_dim,), (right_dim,)), ((), ())), preferred_element_type=F32
    )


def split3(v):
    high = v.astype(BF)
    rest = v - high.astype(F32)
    mid = rest.astype(BF)
    return [high, mid, (rest - mid.astype(F32)).astype(BF)]


def extend(block, columns):
    rows = block.shape[0]
    fill = HEAD_DIM - len(columns)
    return jnp.concatenate([block] + list(columns) + [jnp.zeros((rows, fill), BF)], axis=1)


def unfold(v, start, period):
    return jnp.concatenate(
        [v[:, start : start + HEAD_DIM], v[:, period + start : period + start + HEAD_DIM]], axis=0
    )


def fold(parts):
    rows = parts[0].shape[0] // 2
    return jnp.concatenate([p[:rows] for p in parts] + [p[rows:] for p in parts], axis=1)


def spread_keys(index, qkv_ref, text_ref, bias_ref, text_bias_ref, outs, key_ones, value_ones):
    wide = text_ref.shape[1] // 2
    at = index * HEAD_DIM
    sources = (
        (unfold(qkv_ref, HEAD_DIM, 3 * HEAD_DIM), unfold(qkv_ref, 2 * HEAD_DIM, 3 * HEAD_DIM), bias_ref),
        (text_ref[:, at : at + HEAD_DIM], text_ref[:, wide + at : wide + at + HEAD_DIM], text_bias_ref),
    )
    for i, (keys, values, bias) in enumerate(sources):
        one = jnp.ones((keys.shape[0], 1), BF)
        outs[2 * i][...] = extend(keys, [bias[...]] + [one] * key_ones)
        outs[2 * i + 1][...] = extend(values, [one] * value_ones)


def attend_forward_kernel(
    index, qkv_ref, text_ref, bias_ref, text_bias_ref, gate_ref, q_ref,
    mixed_ref, own_ref, cross_ref, lse_ref, *spread
):
    @pl.when(pl.program_id(0) == 0)
    def _():
        spread_keys(index, qkv_ref, text_ref, bias_ref, text_bias_ref, spread, 0, 1)

    query = unfold(q_ref, 0, 3 * HEAD_DIM) * SCALE
    query = extend(query, [jnp.ones((query.shape[0], 1), BF)])

    def soft(keys, values):
        scores = contract(query, keys[...], 1, 1)
        high = jnp.max(scores, axis=1, keepdims=True)
        total = contract(jnp.exp(scores - high).astype(BF), values[...], 1, 0)
        mass = total[:, HEAD_DIM : HEAD_DIM + 1]
        return total[:, :HEAD_DIM] / mass, high + jnp.log(mass)

    own, own_lse = soft(spread[0], spread[1])
    cross, cross_lse = soft(spread[2], spread[3])
    own_ref[...] = fold([own])
    cross_ref[...] = fold([cross])
    mixed_ref[...] = fold([own + gate_ref[...] * cross]).astype(BF)
    lse_ref[...] = fold([own_lse, cross_lse])


def attend_backward_kernel(
    index, qkv_ref, text_ref, bias_ref, text_bias_ref, gate_ref, q_ref, up_ref, own_ref, cross_ref, lse_ref,
    grad_ref, dtext_ref, dgate_ref, *scratch
):
    spread, sums = scratch[:4], scratch[4:]
    step = pl.program_id(0)

    @pl.when(step == 0)
    def _():
        spread_keys(index, qkv_ref, text_ref, bias_ref, text_bias_ref, spread, 3, 3)
        for ref in sums + (dgate_ref,):
            ref[...] = jnp.zeros_like(ref)

    query = unfold(q_ref, 0, 3 * HEAD_DIM)
    one = jnp.ones((query.shape[0], 1), BF)
    up = unfold(up_ref, 0, HEAD_DIM)
    cross = unfold(cross_ref, 0, HEAD_DIM)
    up_float = up.astype(F32)
    up_cross = (gate_ref[...] * up_float).astype(BF)
    dgate_ref[...] += jnp.sum(up_float * cross, axis=0, keepdims=True)
    half = lse_ref.shape[0]
    lse = jnp.concatenate([lse_ref[:, 0:2], lse_ref[:, 2:4]], axis=0)

    def one_soft(upstream, row, spread_lse, keys, values, key_sum, value_sum):
        center = jnp.sum(row, axis=1, keepdims=True)
        left = extend(query * SCALE, [one] + [-part for part in split3(spread_lse)])
        weights = jnp.exp(contract(left, keys[...], 1, 1))
        left = extend(upstream, [-part for part in split3(center)])
        score_grad = (weights * contract(left, values[...], 1, 1)).astype(BF)
        weights = weights.astype(BF)
        key_sum[...] += contract(score_grad, query, 0, 0)
        value_sum[...] += contract(weights, upstream, 0, 0)
        return contract(score_grad, keys[...], 1, 0)[:, :HEAD_DIM]

    dq = one_soft(
        up, up_float * unfold(own_ref, 0, HEAD_DIM), lse[:, 0:1], spread[0], spread[1], sums[0], sums[1]
    )
    dq += one_soft(
        up_cross, up_cross.astype(F32) * cross, lse[:, 1:2], spread[2], spread[3], sums[2], sums[3]
    )
    dq = (dq * SCALE).astype(BF)
    here = pl.ds(pl.multiple_of(step * half, half), half)
    grad_ref[here, 0:HEAD_DIM] = dq[:half]
    grad_ref[here, 3 * HEAD_DIM : 4 * HEAD_DIM] = dq[half:]

    @pl.when(step == pl.num_programs(0) - 1)
    def _():
        slots = grad_ref.shape[0]
        both = jnp.concatenate([sums[0][...] * SCALE, sums[1][...]], axis=1).astype(BF)
        grad_ref[:, HEAD_DIM : 3 * HEAD_DIM] = both[:slots]
        grad_ref[:, 4 * HEAD_DIM :] = both[slots:]
        dtext_ref[...] = jnp.concatenate([sums[2][...] * SCALE, sums[3][...]], axis=1).astype(BF)


def whole_block(shape):
    return pl.BlockSpec(shape, lambda i: (0,) * len(shape), pipeline_mode=pl.Buffered(1))


def row_block(rows, columns):
    return pl.BlockSpec((rows, columns), lambda i: (i, 0))


def params():
    return pltpu.CompilerParams(vmem_limit_bytes=VMEM_BYTES)


def cost(flops, size, exps=0):
    return pl.CostEstimate(flops=int(flops), bytes_accessed=int(size), transcendentals=int(exps))


def attend_forward(qkv, text, bias, text_bias, gate, index, rows):
    half, words, head = qkv.shape[0], text.shape[0], HEAD_DIM
    slots = 2 * half
    pairs = slots * (slots + words)
    return pl.pallas_call(
        functools.partial(attend_forward_kernel, index),
        grid=(half // rows,),
        in_specs=[
            whole_block((half, 6 * head)), whole_block(text.shape), whole_block((slots, 1)),
            whole_block((words, 1)), whole_block((1, head)), row_block(rows, 6 * head),
        ],
        out_specs=[row_block(rows, 2 * head)] * 3 + [row_block(rows, 4)],
        out_shape=[
            jax.ShapeDtypeStruct((half, 2 * head), BF),
            jax.ShapeDtypeStruct((half, 2 * head), F32),
            jax.ShapeDtypeStruct((half, 2 * head), F32),
            jax.ShapeDtypeStruct((half, 4), F32),
        ],
        scratch_shapes=[pltpu.VMEM((n, 2 * head), BF) for n in (slots, slots, words, words)],
        compiler_params=params(),
        cost_estimate=cost(pairs * head * 16, slots * head * 18, pairs),
        name="attend_forward",
    )(qkv, text, bias, text_bias, gate, qkv)


def attend_backward(qkv, text, bias, text_bias, gate, up, own, cross, lse, index, rows):
    half, words, head = qkv.shape[0], text.shape[0], HEAD_DIM
    slots = 2 * half
    pairs = slots * (slots + words)
    return pl.pallas_call(
        functools.partial(attend_backward_kernel, index),
        grid=(half // rows,),
        in_specs=[
            whole_block((half, 6 * head)), whole_block(text.shape), whole_block((slots, 1)),
            whole_block((words, 1)), whole_block((1, head)), row_block(rows, 6 * head),
            row_block(rows, 2 * head), row_block(rows, 2 * head), row_block(rows, 2 * head), row_block(rows, 4),
        ],
        out_specs=[whole_block((half, 6 * head)), whole_block((words, 2 * head)), whole_block((1, head))],
        out_shape=[
            jax.ShapeDtypeStruct((half, 6 * head), BF),
            jax.ShapeDtypeStruct((words, 2 * head), BF),
            jax.ShapeDtypeStruct((1, head), F32),
        ],
        scratch_shapes=[pltpu.VMEM((n, 2 * head), BF) for n in (slots, slots, words, words)]
        + [pltpu.VMEM((n, head), F32) for n in (slots, slots, words, words)],
        compiler_params=params(),
        cost_estimate=cost(pairs * head * 40, slots * head * 26, pairs),
        name="attend_backward",
    )(qkv, text, bias, text_bias, gate, qkv, up, own, cross, lse)


def swap_halves(v):
    lane = lax.broadcasted_iota(jnp.int32, v.shape, 1)
    half = HEAD_DIM // 2
    return jnp.where(
        lane % HEAD_DIM < half, pltpu.roll(v, LANES - half, 1), pltpu.roll(v, half, 1)
    )


def tiles_of(v):
    return [v[:, t : t + LANES] for t in range(0, v.shape[1], LANES)]


def split_heads(parts, out_refs):
    heads, groups = len(out_refs), out_refs[0].shape[0]
    rows = parts[0].shape[0]
    for g in range(groups):
        for i in range(heads):
            at = (g * heads + i) * HEAD_DIM
            if at < WIDTH:
                out_refs[i][g] = fold([part[:, at : at + HEAD_DIM] for part in parts])
            else:
                out_refs[i][g] = jnp.zeros(out_refs[i].shape[1:], out_refs[i].dtype)


def join_heads(refs, which, count):
    groups, columns = refs[0].shape[0], []
    for g in range(groups):
        for i, ref in enumerate(refs):
            if (g * len(refs) + i) * HEAD_DIM < WIDTH:
                columns.append(unfold(ref.at[g], which * HEAD_DIM, count * HEAD_DIM))
    return jnp.concatenate(columns, axis=1)


def group_kernel(joint_ref, gains_ref, cos_ref, sin_ref, *out_refs):
    cosine, sine = cos_ref[...], sin_ref[...]
    parts = []
    for which in range(2):
        raw = joint_ref[:, which * WIDTH : (which + 1) * WIDTH]
        root = lax.rsqrt(jnp.mean(raw * raw, axis=1, keepdims=True) + EPS)
        scaled = raw * root * gains_ref[which : which + 1, :]
        turned = [tile * cosine + swap_halves(tile) * sine for tile in tiles_of(scaled)]
        parts.append(jnp.concatenate(turned, axis=1).astype(BF))
    parts.append(joint_ref[:, 2 * WIDTH :].astype(BF))
    split_heads(parts, out_refs)


def ungroup_kernel(heads, *refs):
    grad_refs = refs[:heads]
    joint_ref, gains_ref, cos_ref, sin_ref, out_ref, dgain_ref = refs[heads:]
    cosine, sine = cos_ref[...], sin_ref[...]
    for which in range(2):
        cut = slice(which * WIDTH, (which + 1) * WIDTH)
        grad = join_heads(grad_refs, which, 3).astype(F32)
        turned = [tile * cosine - swap_halves(tile) * sine for tile in tiles_of(grad)]
        grad = jnp.concatenate(turned, axis=1)
        raw = joint_ref[:, cut]
        root = lax.rsqrt(jnp.mean(raw * raw, axis=1, keepdims=True) + EPS)
        unit = raw * root
        dgain_ref[which : which + 1, :] = jnp.sum(grad * unit, axis=0, keepdims=True)
        grad = grad * gains_ref[which : which + 1, :]
        grad = root * (grad - unit * jnp.mean(grad * unit, axis=1, keepdims=True))
        out_ref[:, cut] = grad.astype(BF)
    out_ref[:, 2 * WIDTH :] = join_heads(grad_refs, 2, 3)


def split_kernel(value_ref, *out_refs):
    split_heads([value_ref[...]], out_refs)


def join_kernel(*refs):
    refs[-1][...] = join_heads(refs[:-1], 0, 1)


def pack_kernel(*refs):
    out_ref = refs[-1]
    rows = [ref[...] for ref in refs[:-1]]
    rows.append(jnp.zeros((out_ref.shape[0] - len(rows), out_ref.shape[1]), F32))
    out_ref[...] = jnp.concatenate(rows, axis=0)


def simple_call(kernel, out_shape, name, *args):
    size = sum(a.size * a.dtype.itemsize for a in args)
    shapes = out_shape if isinstance(out_shape, list) else [out_shape]
    return pl.pallas_call(
        kernel,
        in_specs=[pl.BlockSpec(memory_space=pltpu.VMEM)] * len(args),
        out_specs=jax.tree.map(lambda _: pl.BlockSpec(memory_space=pltpu.VMEM), out_shape),
        out_shape=out_shape,
        compiler_params=params(),
        cost_estimate=cost(size * 8, size + sum(o.size * o.dtype.itemsize for o in shapes)),
        name=name,
    )(*args)


def local(
    sizes,
    tokens,
    condition,
    caption,
    caption_len,
    image_shape,
    cotangent,
    joint_weight,
    mixer_weight,
    gate_up_weight,
    down_weight,
    text_weight,
    modulation_weight,
    modulation_bias,
    norm_gains,
    head_gates,
):
    n_dp, n_z, n_core = sizes
    everyone = ("dp", "z", "core")
    seq = ("z", "core")
    n_seq = n_z * n_core
    heads = -(-HEADS // n_seq)
    wide = heads * HEAD_DIM
    spare = n_seq * heads - HEADS
    rows = tokens.shape[1]
    slots = -(-rows // 16) * 16
    dp = lax.axis_index("dp")
    core = lax.axis_index("core")
    z_index = lax.axis_index("z")
    seq_index = lax.axis_index(seq)
    device = lax.axis_index(everyone)

    def swap(v, axis, n, k):
        return lax.ppermute(v, axis, [(i, i ^ k) for i in range(n)])

    def tree(parts):
        while len(parts) > 1:
            parts = [parts[i] + parts[i + 1] for i in range(0, len(parts), 2)]
        return parts[0]

    def sum_over(v, axis, n):
        return tree([v] + [swap(v, axis, n, k) for k in range(1, n)])

    soft_cond = jax.nn.silu(condition).astype(BF)
    partial_mods = product(soft_cond, modulation_weight)
    bias_width = modulation_bias.shape[0]
    bias_start = device * bias_width
    with_bias = (
        lax.dynamic_slice_in_dim(partial_mods, bias_start, bias_width, 1) + modulation_bias[None, :]
    )
    partial_mods = lax.dynamic_update_slice_in_dim(partial_mods, with_bias, bias_start, 1)
    mods_width = partial_mods.shape[1]
    gain_rows, gain_width = norm_gains.shape
    own_gains = lax.dynamic_update_slice_in_dim(
        jnp.zeros((gain_rows, WIDTH), F32), norm_gains.astype(F32), device * gain_width, 1
    ).reshape(1, -1)

    def after(v, *others):
        return lax.optimization_barrier((v,) + others)[0]

    def shift_z(v, k):
        return lax.ppermute(v, "z", [(i, (i + k) % n_z) for i in range(n_z)])

    def place(full, part, index):
        return lax.dynamic_update_slice(full, part[None], (index,) + (0,) * part.ndim)


    def gather_line(shard):
        parts = [shift_z(shard, k) for k in range(1, n_z)]

        def arrive(*before):
            line = place(jnp.zeros((n_z,) + shard.shape, shard.dtype), shard, z_index)
            for k, part in enumerate(parts, 1):
                line = place(line, after(part, *before), (z_index - k) % n_z)
            return line.reshape(-1, shard.shape[1])

        return arrive

    def gather_dp(line):
        return lax.all_gather(line, "dp", axis=0, tiled=True)

    def gather_all(shard):
        if n_dp != 4:
            full = lax.all_gather(shard, everyone, axis=0, tiled=True)
            return lambda *before: lambda *before: full
        chunk, columns = shard.shape
        line_arrive = gather_line(shard)

        def first(*before):
            line = line_arrive(*before)
            empty = jnp.zeros((n_dp, n_z, n_core, chunk, columns), shard.dtype)
            line, empty = lax.optimization_barrier((line, empty))
            near = [swap(line, "dp", n_dp, k) for k in (1, 2)]

            def second(*before):
                half = line.shape[0] // 2
                by_x, by_y = [after(v, *before) for v in near]
                far = (swap(by_y[:half], "dp", n_dp, 1), swap(by_x[half:], "dp", n_dp, 2))
                full = empty
                parts = [(line, dp, 0), (by_x, dp ^ 1, 0), (by_y, dp ^ 2, 0)]
                parts += [(far[0], dp ^ 3, 0), (far[1], dp ^ 3, n_z // 2)]
                for part, index, start in parts:
                    for held, of_core in ((part, core), (swap(part, "core", n_core, 1), 1 - core)):
                        held = held.reshape(1, -1, 1, chunk, columns)
                        full = lax.dynamic_update_slice(full, held, (index, start, of_core, 0, 0))
                return full.reshape(-1, columns)

            second.line = line
            return second

        return first

    def reduce_dp(part):
        return lax.psum_scatter(part, "dp", scatter_dimension=0, tiled=True)

    def reduce_line(part):
        line = part.reshape(n_z, -1, part.shape[1])

        def at(index):
            return lax.dynamic_index_in_dim(line, index, 0, keepdims=False)

        others = [shift_z(at((z_index + k) % n_z), k) for k in range(1, n_z)]

        def arrive(*before):
            parts = [at(z_index)] + [after(other, *before) for other in others]
            return tree([v.astype(F32) for v in parts])

        return arrive

    def by_core(mine, other, axis):
        first = jnp.where(core == 0, mine, other)
        second = jnp.where(core == 0, other, mine)
        return jnp.concatenate([first, second], axis=axis)

    def column_split(left, right):
        half = right.shape[1] // n_core
        mine = lax.dynamic_slice_in_dim(right, core * half, half, 1)
        other = lax.dynamic_slice_in_dim(right, (1 - core) * half, half, 1)
        both_right = jnp.concatenate([mine, swap(other, "core", n_core, 1)], axis=0)
        return both_cores(left), both_right

    def both_cores(v):
        return jnp.concatenate([v, swap(v, "core", n_core, 1)], axis=0)

    def sum_cores(v, *before):
        return v[:slots] + after(swap(v[slots:], "core", n_core, 1), *before)

    def own_rows(part):
        return by_core(*trade(part.astype(BF)), 1).astype(F32)

    def core_columns(shard):
        half = shard.shape[1] // n_core
        mine = lax.dynamic_slice_in_dim(shard, core * half, half, 1)
        other = lax.dynamic_slice_in_dim(shard, (1 - core) * half, half, 1)
        return by_core(mine, swap(other, "core", n_core, 1), 0)

    def grad_of(left, right):
        return contract(left, right, 0, 0).astype(BF)

    def trade(part):
        count = part.shape[0] // n_core
        kept = lax.dynamic_slice_in_dim(part, core * count, count, 0)
        sent = lax.dynamic_slice_in_dim(part, (1 - core) * count, count, 0)
        return kept, swap(sent, "core", n_core, 1)

    flat_text = caption.reshape(-1, caption.shape[2])
    text_left, text_right = column_split(flat_text.T, text_weight)
    def halve(v):
        count = n_dp
        while count > 1:
            count //= 2
            bit = (dp // count) % 2
            kept = lax.dynamic_slice_in_dim(v, bit * count, count, 0)
            sent = lax.dynamic_slice_in_dim(v, (1 - bit) * count, count, 0)
            v = kept + swap(sent, "dp", n_dp, count)
        return v

    def double(v, axis, n):
        k = 1
        while k < n:
            v = v + swap(v, axis, n, k)
            k *= 2
        return v

    head_rows = jnp.concatenate(
        [partial_mods, jnp.broadcast_to(own_gains, (n_dp, own_gains.shape[1]))], axis=1
    )
    head_vector = double(double(halve(after(head_rows, text_right)), "core", n_core), "z", n_z)
    mods = head_vector[:, :mods_width]
    gains = head_vector[0, mods_width:].reshape(gain_rows, WIDTH)
    shift_a, scale_a, gate_a, shift_f, scale_f, gate_f = [
        mods[:, i * WIDTH : (i + 1) * WIDTH] for i in range(6)
    ]
    gain = [gains[i : i + 1] for i in range(gain_rows)]

    own_units = down_weight.shape[0]
    unit_blocks = n_dp * n_z
    shard_rows = gate_up_weight.shape[0]
    by_units = gate_up_weight.reshape(shard_rows, 2 * unit_blocks, n_core, own_units)


    def units_of(which):
        return lax.dynamic_index_in_dim(by_units, which, 2, keepdims=False).reshape(shard_rows, -1)

    gate_up_shard = by_core(units_of(core), swap(after(units_of(1 - core), mods), "core", n_core, 1), 0)
    text_part = grad_of(text_left, text_right)
    text_sum = lax.psum_scatter(text_part, ("dp", "z"), scatter_dimension=0, tiled=True)
    joint_near = gather_all(joint_weight)(text_part)
    joint_line = getattr(joint_near, "line", text_part)
    first_shard = jnp.concatenate([gate_up_shard, core_columns(after(mixer_weight, mods))], axis=1)
    first_line = gather_line(after(first_shard, joint_line))

    pad = ((0, slots - rows), (0, 0))
    xfloat = jnp.pad(tokens[0], pad).astype(F32)
    upstream = jnp.pad(cotangent[0], pad).astype(F32)
    normed_in, normed_pull = jax.vjp(modulate, xfloat, gain[0], scale_a, shift_a)
    normed_low = normed_in.astype(BF)
    joint_full = joint_near(normed_low)
    joint = product(normed_low, joint_full)
    def to_groups(parts):
        count = parts[0].shape[0]
        spread = []
        for part in parts:
            part = jnp.pad(part, ((0, 0), (0, spare * HEAD_DIM)))
            spread.append(part.reshape(count, n_seq, wide).transpose(1, 0, 2))
        return jnp.concatenate(spread, axis=2)

    def from_groups(part):
        part = part.transpose(1, 0, 2)
        return part.reshape(part.shape[0], n_seq * wide)[:, :WIDTH]

    def exchange(v):
        return lax.all_to_all(v, seq, 0, 0, tiled=True)

    lane = jnp.arange(LANES)
    freq = jnp.exp((lane % (HEAD_DIM // 2)).astype(F32) * (-jnp.log(10000.0) / (HEAD_DIM // 2)))
    angle = (seq_index * rows + jnp.arange(slots)).astype(F32)[:, None] * freq[None, :]
    cosine = jnp.cos(angle)
    sine = jnp.sin(angle) * jnp.where(lane % HEAD_DIM < HEAD_DIM // 2, -1.0, 1.0)[None, :]
    rope_gains = gains[4:6]
    half_slots = slots // 2

    def head_arrays(columns):
        return [jax.ShapeDtypeStruct((n_seq, half_slots, columns * HEAD_DIM), BF)] * heads

    def exchange_heads(arrays):
        return [exchange(v).reshape(n_seq * half_slots, -1) for v in arrays]

    def exchange_back(arrays):
        return [exchange(v.reshape(n_seq, half_slots, -1)) for v in arrays]

    sent = simple_call(group_kernel, head_arrays(6), "group_heads", joint, rope_gains, cosine, sine)
    first_line = first_line(sent[0])
    split_at = gate_up_shard.shape[1]
    mixer_half = gather_dp(first_line[:, split_at:])
    gate_up_half = gather_dp(first_line[:, :split_at])
    down_line = gather_line(after(down_weight, first_line))
    text_raw = own_rows(after(text_sum, sent[0]))
    text_rows = text_raw.shape[0]
    text_keys, text_key_pull = jax.vjp(norm_rows, text_raw[:, :WIDTH], gain[6])
    text_own = exchange(
        to_groups([text_keys.astype(BF), text_raw[:, WIDTH:].astype(BF)])
    ).reshape(n_seq * text_rows, 2 * wide)

    qkv = exchange_heads(sent)
    mixer_full = by_core(mixer_half, swap(mixer_half, "core", n_core, 1), 1)
    down_half = gather_dp(down_line(qkv[0]))
    slot = jnp.arange(n_seq * slots)
    side, line = slot // (n_seq * half_slots), slot % (n_seq * half_slots)
    within = side * half_slots + line % half_slots
    shape_row = image_shape[dp]
    valid = shape_row[0] * (shape_row[1] + 1)
    live = (within < rows) & ((line // half_slots) * rows + within < valid)
    bias = jnp.where(live, 0.0, NEG).astype(BF)[:, None]
    text_bias = jnp.where(jnp.arange(TEXT) < caption_len[dp], 0.0, NEG).astype(BF)[:, None]
    tanh_gates = jnp.tanh(head_gates)
    first_head = seq_index * heads
    own_gates = lax.dynamic_slice_in_dim(jnp.pad(tanh_gates, (0, spare)), first_head, heads, 0)
    gate_rows = [jnp.broadcast_to(own_gates[i : i + 1, None], (1, HEAD_DIM)) for i in range(heads)]
    attended = [
        attend_forward(qkv[i], text_own, bias, text_bias, gate_rows[i], i, 2 * half_slots)
        for i in range(heads)
    ]
    token_shape = jax.ShapeDtypeStruct((slots, WIDTH), BF)
    mixed = simple_call(
        join_kernel, token_shape, "join_heads", *exchange_back([v[0] for v in attended])
    )
    proj = product(mixed, mixer_full)
    branch_a, branch_a_pull = jax.vjp(branch_out, proj, gain[1], gate_a)
    hstate = xfloat + branch_a
    ffn_in, ffn_in_pull = jax.vjp(modulate, hstate, gain[2], scale_f, shift_f)

    ffn_both = both_cores(ffn_in.astype(BF))
    gate_up = product(ffn_both, gate_up_half)
    hidden, swiglu_pull = jax.vjp(swiglu, gate_up)
    hidden_low = hidden.astype(BF)
    ffn = sum_cores(product(hidden_low, down_half))
    branch_f, branch_f_pull = jax.vjp(branch_out, ffn, gain[3], gate_f)
    output = (hstate + branch_f).astype(BF)[None, :rows]

    ffn_grad, gain3_grad, gate_f_grad = branch_f_pull(upstream)
    ffn_grad_both = both_cores(ffn_grad.astype(BF))
    (gate_up_grad_rows,) = swiglu_pull(contract(ffn_grad_both, down_half, 1, 1))
    gate_up_low = gate_up_grad_rows.astype(BF)
    down_part = grad_of(hidden_low, ffn_grad_both)
    gate_up_part = grad_of(ffn_both, after(gate_up_low, down_part))
    down_part = reduce_dp(down_part)
    state_part, gain2_grad, scale_f_grad, shift_f_grad = ffn_in_pull(
        sum_cores(contract(gate_up_low, gate_up_half, 1, 1), gate_up_part)
    )
    state_grad = upstream + state_part
    proj_grad, gain1_grad, gate_a_grad = branch_a_pull(state_grad)
    proj_low = proj_grad.astype(BF)
    mixed_grad = contract(proj_low, mixer_full, 1, 1).astype(BF)
    ups = exchange_heads(simple_call(split_kernel, head_arrays(2), "split_heads", mixed_grad))
    mixer_part = grad_of(*column_split(mixed, after(proj_low, mixed_grad)))
    ups[0] = after(ups[0], mixer_part)
    gate_up_part = reduce_dp(after(gate_up_part, mixer_part))
    mixer_part = reduce_dp(mixer_part)
    ups[-1] = after(ups[-1], down_part)
    grads, dtexts, dgates = zip(*[
        attend_backward(
            qkv[i], text_own, bias, text_bias, gate_rows[i], ups[i], *attended[i][1:], i, 2 * half_slots
        )
        for i in range(heads)
    ])
    grouped = exchange_back(grads)
    down_line = reduce_line(after(down_part, grads[0]))
    mixer_line = reduce_line(after(mixer_part, grads[-1]))
    joint_low, rope_gain_grads = simple_call(
        functools.partial(ungroup_kernel, heads),
        [jax.ShapeDtypeStruct((slots, 3 * WIDTH), BF), jax.ShapeDtypeStruct((2, WIDTH), F32)],
        "ungroup_heads", *grouped, joint, rope_gains, cosine, sine,
    )
    joint_left, joint_right = column_split(normed_low, joint_low)
    piece = joint_right.shape[1] // 2
    joint_parts = [grad_of(joint_left, joint_right[:, p * piece : (p + 1) * piece]) for p in range(2)]
    joint_lines = [
        reduce_line(reduce_dp(after(part, gate_up_part, mixer_part))) for part in joint_parts
    ]
    later_low = after(joint_low, *joint_parts)
    input_part, gain0_grad, scale_a_grad, shift_a_grad = normed_pull(
        contract(later_low, joint_full, 1, 1)
    )
    gate_up_line = reduce_line(after(gate_up_part, later_low))
    down_out = down_line(later_low)
    mixer_out = own_rows(mixer_line(later_low))
    joint_out = own_rows(jnp.concatenate([arrive(input_part) for arrive in joint_lines], axis=1))
    kept, received = [
        v.reshape(shard_rows, 2 * unit_blocks, 1, own_units)
        for v in trade(gate_up_line(input_part).astype(BF))
    ]
    gate_up_out = by_core(kept, received, 2).reshape(shard_rows, -1).astype(F32)
    tokens_grad = (state_grad + input_part).astype(BF)[None, :rows]
    dtext = jnp.concatenate([v[:, :HEAD_DIM] for v in dtexts] + [v[:, HEAD_DIM:] for v in dtexts], axis=1)
    text_back = exchange(dtext.reshape(n_seq, text_rows, 2 * wide))
    text_key_grad, gain6_grad = text_key_pull(from_groups(text_back[:, :, :wide]).astype(F32))
    text_grad_rows = jnp.concatenate(
        [text_key_grad.astype(BF), from_groups(text_back[:, :, wide:])], axis=1
    )
    text_grad_all = lax.all_gather(after(text_grad_rows, *joint_parts), everyone, axis=0, tiled=True)
    text_grad = contract(flat_text, text_grad_all, 0, 0)

    gates_own = jnp.concatenate([jnp.sum(v, axis=1) for v in dgates]) * (1.0 - own_gates * own_gates)
    gates_all = lax.dynamic_update_slice_in_dim(jnp.zeros((WIDTH,), F32), gates_own, first_head, 0)[None, :]
    pieces = [shift_a_grad, scale_a_grad, gate_a_grad, shift_f_grad, scale_f_grad, gate_f_grad]
    shared = [
        gain0_grad, gain1_grad, gain2_grad, gain3_grad, rope_gain_grads[0:1], rope_gain_grads[1:2], gain6_grad,
    ]
    tail = pieces + shared + [gates_all]
    tail = simple_call(
        pack_kernel, jax.ShapeDtypeStruct((-(-len(tail) // 8) * 8, WIDTH), F32), "pack_rows", *tail
    )
    tail = sum_over(sum_over(tail, "core", n_core), "z", n_z)
    tails = [tail] + [swap(tail, "dp", n_dp, k) for k in range(1, n_dp)]
    count = len(pieces)
    total = tree([t[count:] for t in tails])
    gates_grad = total[gain_rows, :HEADS]
    gains_grad = lax.dynamic_slice_in_dim(total[:gain_rows], device * gain_width, gain_width, 1)
    mods_low = jnp.stack([t[:count].astype(BF).reshape(-1) for t in tails])
    cond_rows = jnp.concatenate(
        [lax.dynamic_slice_in_dim(soft_cond, dp ^ k, 1, 0) for k in range(n_dp)], axis=0
    )
    modulation_grad = contract(cond_rows, mods_low, 0, 0)
    bias_grad = lax.dynamic_slice_in_dim(
        jnp.sum(mods_low.astype(F32), axis=0), bias_start, bias_width, 0
    )
    return (
        output,
        tokens_grad,
        joint_out,
        mixer_out,
        gate_up_out,
        down_out,
        text_grad,
        modulation_grad,
        bias_grad,
        gains_grad,
        gates_grad,
    )


def solution(mesh):
    n_dp, n_seq = mesh.shape["dp"], mesh.shape["seq"]
    sizes = (n_dp, n_seq // 2, 2)
    split = Mesh(mesh.devices.reshape(sizes), ("dp", "z", "core"))
    seq, everyone = ("z", "core"), ("dp", "z", "core")
    token_spec, row_spec, column_spec = P("dp", seq, None), P(everyone, None), P(None, everyone)
    in_specs = (
        token_spec, column_spec, P(None, None, everyone), P(), P(), token_spec,
        row_spec, row_spec, row_spec, row_spec, row_spec, row_spec, P(everyone), column_spec, P(),
    )
    out_specs = (
        token_spec, token_spec, row_spec, row_spec, row_spec, row_spec, row_spec, row_spec,
        P(everyone), column_spec, P(),
    )
    return jax.shard_map(
        functools.partial(local, sizes), mesh=split, in_specs=in_specs, out_specs=out_specs, check_vma=False
    )
```

```python
import functools

import jax
import jax.numpy as jnp
from jax import lax
from jax.experimental import pallas as pl
from jax.experimental.pallas import tpu as pltpu
from jax.sharding import Mesh
from jax.sharding import PartitionSpec as P

HEADS = 24
HEAD_DIM = 64
TEXT = 256
WIDTH = HEADS * HEAD_DIM
EPS = 1e-06
NEG = -1e30
SCALE = float(HEAD_DIM) ** (-0.5)
LANES = 128
BF = jnp.bfloat16
F32 = jnp.float32
VMEM_BYTES = 56 << 20


def norm_rows(v, gain):
    return v * lax.rsqrt(jnp.mean(v * v, axis=-1, keepdims=True) + EPS) * gain


def modulate(v, gain, scale, shift):
    return norm_rows(v, gain) * (1.0 + scale) + shift


def branch_out(v, gain, gate):
    return gate * norm_rows(v, gain)


def swiglu(gate_up):
    half = gate_up.shape[-1] // 2
    return jax.nn.silu(gate_up[:, :half]) * gate_up[:, half:]


def product(left, right):
    return jnp.dot(left, right, preferred_element_type=F32)


def contract(left, right, left_dim, right_dim):
    return lax.dot_general(
        left, right, (((left_dim,), (right_dim,)), ((), ())), preferred_element_type=F32
    )


def split3(v):
    high = v.astype(BF)
    rest = v - high.astype(F32)
    mid = rest.astype(BF)
    return [high, mid, (rest - mid.astype(F32)).astype(BF)]


def extend(block, columns):
    rows = block.shape[0]
    fill = HEAD_DIM - len(columns)
    return jnp.concatenate([block] + list(columns) + [jnp.zeros((rows, fill), BF)], axis=1)


def unfold(v, start, period):
    return jnp.concatenate(
        [v[:, start : start + HEAD_DIM], v[:, period + start : period + start + HEAD_DIM]], axis=0
    )


def fold(parts):
    rows = parts[0].shape[0] // 2
    return jnp.concatenate([p[:rows] for p in parts] + [p[rows:] for p in parts], axis=1)


def spread_keys(index, qkv_ref, text_ref, bias_ref, text_bias_ref, outs, key_ones, value_ones):
    wide = text_ref.shape[1] // 2
    at = index * HEAD_DIM
    sources = (
        (unfold(qkv_ref, HEAD_DIM, 3 * HEAD_DIM), unfold(qkv_ref, 2 * HEAD_DIM, 3 * HEAD_DIM), bias_ref),
        (text_ref[:, at : at + HEAD_DIM], text_ref[:, wide + at : wide + at + HEAD_DIM], text_bias_ref),
    )
    for i, (keys, values, bias) in enumerate(sources):
        one = jnp.ones((keys.shape[0], 1), BF)
        outs[2 * i][...] = extend(keys, [bias[...]] + [one] * key_ones)
        outs[2 * i + 1][...] = extend(values, [one] * value_ones)


def attend_forward_kernel(
    index, qkv_ref, text_ref, bias_ref, text_bias_ref, gate_ref, q_ref,
    mixed_ref, own_ref, cross_ref, lse_ref, *spread
):
    @pl.when(pl.program_id(0) == 0)
    def _():
        spread_keys(index, qkv_ref, text_ref, bias_ref, text_bias_ref, spread, 0, 1)

    query = unfold(q_ref, 0, 3 * HEAD_DIM) * SCALE
    query = extend(query, [jnp.ones((query.shape[0], 1), BF)])

    def soft(keys, values):
        scores = contract(query, keys[...], 1, 1)
        high = jnp.max(scores, axis=1, keepdims=True)
        total = contract(jnp.exp(scores - high).astype(BF), values[...], 1, 0)
        mass = total[:, HEAD_DIM : HEAD_DIM + 1]
        return total[:, :HEAD_DIM] / mass, high + jnp.log(mass)

    own, own_lse = soft(spread[0], spread[1])
    cross, cross_lse = soft(spread[2], spread[3])
    own_ref[...] = fold([own])
    cross_ref[...] = fold([cross])
    mixed_ref[...] = fold([own + gate_ref[...] * cross]).astype(BF)
    lse_ref[...] = fold([own_lse, cross_lse])


def attend_backward_kernel(
    index, qkv_ref, text_ref, bias_ref, text_bias_ref, gate_ref, q_ref, up_ref, own_ref, cross_ref, lse_ref,
    grad_ref, dtext_ref, dgate_ref, *scratch
):
    spread, sums = scratch[:4], scratch[4:]
    step = pl.program_id(0)

    @pl.when(step == 0)
    def _():
        spread_keys(index, qkv_ref, text_ref, bias_ref, text_bias_ref, spread, 3, 3)
        for ref in sums + (dgate_ref,):
            ref[...] = jnp.zeros_like(ref)

    query = unfold(q_ref, 0, 3 * HEAD_DIM)
    one = jnp.ones((query.shape[0], 1), BF)
    up = unfold(up_ref, 0, HEAD_DIM)
    cross = unfold(cross_ref, 0, HEAD_DIM)
    up_float = up.astype(F32)
    up_cross = (gate_ref[...] * up_float).astype(BF)
    dgate_ref[...] += jnp.sum(up_float * cross, axis=0, keepdims=True)
    half = lse_ref.shape[0]
    lse = jnp.concatenate([lse_ref[:, 0:2], lse_ref[:, 2:4]], axis=0)

    def one_soft(upstream, row, spread_lse, keys, values, key_sum, value_sum):
        center = jnp.sum(row, axis=1, keepdims=True)
        left = extend(query * SCALE, [one] + [-part for part in split3(spread_lse)])
        weights = jnp.exp(contract(left, keys[...], 1, 1))
        left = extend(upstream, [-part for part in split3(center)])
        score_grad = (weights * contract(left, values[...], 1, 1)).astype(BF)
        weights = weights.astype(BF)
        key_sum[...] += contract(score_grad, query, 0, 0)
        value_sum[...] += contract(weights, upstream, 0, 0)
        return contract(score_grad, keys[...], 1, 0)[:, :HEAD_DIM]

    dq = one_soft(
        up, up_float * unfold(own_ref, 0, HEAD_DIM), lse[:, 0:1], spread[0], spread[1], sums[0], sums[1]
    )
    dq += one_soft(
        up_cross, up_cross.astype(F32) * cross, lse[:, 1:2], spread[2], spread[3], sums[2], sums[3]
    )
    dq = (dq * SCALE).astype(BF)
    here = pl.ds(pl.multiple_of(step * half, half), half)
    grad_ref[here, 0:HEAD_DIM] = dq[:half]
    grad_ref[here, 3 * HEAD_DIM : 4 * HEAD_DIM] = dq[half:]

    @pl.when(step == pl.num_programs(0) - 1)
    def _():
        slots = grad_ref.shape[0]
        both = jnp.concatenate([sums[0][...] * SCALE, sums[1][...]], axis=1).astype(BF)
        grad_ref[:, HEAD_DIM : 3 * HEAD_DIM] = both[:slots]
        grad_ref[:, 4 * HEAD_DIM :] = both[slots:]
        dtext_ref[...] = jnp.concatenate([sums[2][...] * SCALE, sums[3][...]], axis=1).astype(BF)


def whole_block(shape):
    return pl.BlockSpec(shape, lambda i: (0,) * len(shape), pipeline_mode=pl.Buffered(1))


def row_block(rows, columns):
    return pl.BlockSpec((rows, columns), lambda i: (i, 0))


def params():
    return pltpu.CompilerParams(vmem_limit_bytes=VMEM_BYTES)


def cost(flops, size, exps=0):
    return pl.CostEstimate(flops=int(flops), bytes_accessed=int(size), transcendentals=int(exps))


def attend_forward(qkv, text, bias, text_bias, gate, index, rows):
    half, words, head = qkv.shape[0], text.shape[0], HEAD_DIM
    slots = 2 * half
    pairs = slots * (slots + words)
    return pl.pallas_call(
        functools.partial(attend_forward_kernel, index),
        grid=(half // rows,),
        in_specs=[
            whole_block((half, 6 * head)), whole_block(text.shape), whole_block((slots, 1)),
            whole_block((words, 1)), whole_block((1, head)), row_block(rows, 6 * head),
        ],
        out_specs=[row_block(rows, 2 * head)] * 3 + [row_block(rows, 4)],
        out_shape=[
            jax.ShapeDtypeStruct((half, 2 * head), BF),
            jax.ShapeDtypeStruct((half, 2 * head), F32),
            jax.ShapeDtypeStruct((half, 2 * head), F32),
            jax.ShapeDtypeStruct((half, 4), F32),
        ],
        scratch_shapes=[pltpu.VMEM((n, 2 * head), BF) for n in (slots, slots, words, words)],
        compiler_params=params(),
        cost_estimate=cost(pairs * head * 16, slots * head * 18, pairs),
        name="attend_forward",
    )(qkv, text, bias, text_bias, gate, qkv)


def attend_backward(qkv, text, bias, text_bias, gate, up, own, cross, lse, index, rows):
    half, words, head = qkv.shape[0], text.shape[0], HEAD_DIM
    slots = 2 * half
    pairs = slots * (slots + words)
    return pl.pallas_call(
        functools.partial(attend_backward_kernel, index),
        grid=(half // rows,),
        in_specs=[
            whole_block((half, 6 * head)), whole_block(text.shape), whole_block((slots, 1)),
            whole_block((words, 1)), whole_block((1, head)), row_block(rows, 6 * head),
            row_block(rows, 2 * head), row_block(rows, 2 * head), row_block(rows, 2 * head), row_block(rows, 4),
        ],
        out_specs=[whole_block((half, 6 * head)), whole_block((words, 2 * head)), whole_block((1, head))],
        out_shape=[
            jax.ShapeDtypeStruct((half, 6 * head), BF),
            jax.ShapeDtypeStruct((words, 2 * head), BF),
            jax.ShapeDtypeStruct((1, head), F32),
        ],
        scratch_shapes=[pltpu.VMEM((n, 2 * head), BF) for n in (slots, slots, words, words)]
        + [pltpu.VMEM((n, head), F32) for n in (slots, slots, words, words)],
        compiler_params=params(),
        cost_estimate=cost(pairs * head * 40, slots * head * 26, pairs),
        name="attend_backward",
    )(qkv, text, bias, text_bias, gate, qkv, up, own, cross, lse)


def swap_halves(v):
    lane = lax.broadcasted_iota(jnp.int32, v.shape, 1)
    half = HEAD_DIM // 2
    return jnp.where(
        lane % HEAD_DIM < half, pltpu.roll(v, LANES - half, 1), pltpu.roll(v, half, 1)
    )


def tiles_of(v):
    return [v[:, t : t + LANES] for t in range(0, v.shape[1], LANES)]


def split_heads(parts, out_refs):
    heads, groups = len(out_refs), out_refs[0].shape[0]
    rows = parts[0].shape[0]
    for g in range(groups):
        for i in range(heads):
            at = (g * heads + i) * HEAD_DIM
            if at < WIDTH:
                out_refs[i][g] = fold([part[:, at : at + HEAD_DIM] for part in parts])
            else:
                out_refs[i][g] = jnp.zeros(out_refs[i].shape[1:], out_refs[i].dtype)


def join_heads(refs, which, count):
    groups, columns = refs[0].shape[0], []
    for g in range(groups):
        for i, ref in enumerate(refs):
            if (g * len(refs) + i) * HEAD_DIM < WIDTH:
                columns.append(unfold(ref.at[g], which * HEAD_DIM, count * HEAD_DIM))
    return jnp.concatenate(columns, axis=1)


def group_kernel(joint_ref, gains_ref, cos_ref, sin_ref, *out_refs):
    cosine, sine = cos_ref[...], sin_ref[...]
    parts = []
    for which in range(2):
        raw = joint_ref[:, which * WIDTH : (which + 1) * WIDTH]
        root = lax.rsqrt(jnp.mean(raw * raw, axis=1, keepdims=True) + EPS)
        scaled = raw * root * gains_ref[which : which + 1, :]
        turned = [tile * cosine + swap_halves(tile) * sine for tile in tiles_of(scaled)]
        parts.append(jnp.concatenate(turned, axis=1).astype(BF))
    parts.append(joint_ref[:, 2 * WIDTH :].astype(BF))
    split_heads(parts, out_refs)


def ungroup_kernel(heads, *refs):
    grad_refs = refs[:heads]
    joint_ref, gains_ref, cos_ref, sin_ref, out_ref, dgain_ref = refs[heads:]
    cosine, sine = cos_ref[...], sin_ref[...]
    for which in range(2):
        cut = slice(which * WIDTH, (which + 1) * WIDTH)
        grad = join_heads(grad_refs, which, 3).astype(F32)
        turned = [tile * cosine - swap_halves(tile) * sine for tile in tiles_of(grad)]
        grad = jnp.concatenate(turned, axis=1)
        raw = joint_ref[:, cut]
        root = lax.rsqrt(jnp.mean(raw * raw, axis=1, keepdims=True) + EPS)
        unit = raw * root
        dgain_ref[which : which + 1, :] = jnp.sum(grad * unit, axis=0, keepdims=True)
        grad = grad * gains_ref[which : which + 1, :]
        grad = root * (grad - unit * jnp.mean(grad * unit, axis=1, keepdims=True))
        out_ref[:, cut] = grad.astype(BF)
    out_ref[:, 2 * WIDTH :] = join_heads(grad_refs, 2, 3)


def split_kernel(value_ref, *out_refs):
    split_heads([value_ref[...]], out_refs)


def join_kernel(*refs):
    refs[-1][...] = join_heads(refs[:-1], 0, 1)


def pack_kernel(*refs):
    out_ref = refs[-1]
    rows = [ref[...] for ref in refs[:-1]]
    rows.append(jnp.zeros((out_ref.shape[0] - len(rows), out_ref.shape[1]), F32))
    out_ref[...] = jnp.concatenate(rows, axis=0)


def simple_call(kernel, out_shape, name, *args):
    size = sum(a.size * a.dtype.itemsize for a in args)
    shapes = out_shape if isinstance(out_shape, list) else [out_shape]
    return pl.pallas_call(
        kernel,
        in_specs=[pl.BlockSpec(memory_space=pltpu.VMEM)] * len(args),
        out_specs=jax.tree.map(lambda _: pl.BlockSpec(memory_space=pltpu.VMEM), out_shape),
        out_shape=out_shape,
        compiler_params=params(),
        cost_estimate=cost(size * 8, size + sum(o.size * o.dtype.itemsize for o in shapes)),
        name=name,
    )(*args)


def local(
    sizes,
    tokens,
    condition,
    caption,
    caption_len,
    image_shape,
    cotangent,
    joint_weight,
    mixer_weight,
    gate_up_weight,
    down_weight,
    text_weight,
    modulation_weight,
    modulation_bias,
    norm_gains,
    head_gates,
):
    n_dp, n_z, n_core = sizes
    everyone = ("dp", "z", "core")
    seq = ("z", "core")
    n_seq = n_z * n_core
    heads = -(-HEADS // n_seq)
    wide = heads * HEAD_DIM
    spare = n_seq * heads - HEADS
    rows = tokens.shape[1]
    slots = -(-rows // 16) * 16
    dp = lax.axis_index("dp")
    core = lax.axis_index("core")
    z_index = lax.axis_index("z")
    seq_index = lax.axis_index(seq)
    device = lax.axis_index(everyone)

    def swap(v, axis, n, k):
        return lax.ppermute(v, axis, [(i, i ^ k) for i in range(n)])

    def tree(parts):
        while len(parts) > 1:
            parts = [parts[i] + parts[i + 1] for i in range(0, len(parts), 2)]
        return parts[0]

    def sum_over(v, axis, n):
        return tree([v] + [swap(v, axis, n, k) for k in range(1, n)])

    soft_cond = jax.nn.silu(condition).astype(BF)
    partial_mods = product(soft_cond, modulation_weight)
    bias_width = modulation_bias.shape[0]
    bias_start = device * bias_width
    with_bias = (
        lax.dynamic_slice_in_dim(partial_mods, bias_start, bias_width, 1) + modulation_bias[None, :]
    )
    partial_mods = lax.dynamic_update_slice_in_dim(partial_mods, with_bias, bias_start, 1)
    mods_width = partial_mods.shape[1]
    gain_rows, gain_width = norm_gains.shape
    own_gains = lax.dynamic_update_slice_in_dim(
        jnp.zeros((gain_rows, WIDTH), F32), norm_gains.astype(F32), device * gain_width, 1
    ).reshape(1, -1)

    def after(v, *others):
        return lax.optimization_barrier((v,) + others)[0]

    def shift_z(v, k):
        return lax.ppermute(v, "z", [(i, (i + k) % n_z) for i in range(n_z)])

    def place(full, part, index):
        return lax.dynamic_update_slice(full, part[None], (index,) + (0,) * part.ndim)


    def gather_line(shard):
        parts = [shift_z(shard, k) for k in range(1, n_z)]

        def arrive(*before):
            line = place(jnp.zeros((n_z,) + shard.shape, shard.dtype), shard, z_index)
            for k, part in enumerate(parts, 1):
                line = place(line, after(part, *before), (z_index - k) % n_z)
            return line.reshape(-1, shard.shape[1])

        return arrive

    class Gather:
        def __init__(self, shard):
            self.stack, self.offsets, self.next = shard[None], [0], n_z // 2
            self.send()

        def send(self):
            self.pending = swap(self.stack, "z", n_z, self.next) if self.next else None

        def step(self, *before):
            other = after(self.pending, *before)
            self.offsets = self.offsets + [offset ^ self.next for offset in self.offsets]
            self.stack = jnp.concatenate([self.stack, other], axis=0)
            self.next //= 2
            self.send()
            return self.stack

        def finish(self, *before):
            while self.next > 1:
                self.step(*before)
            count = len(self.offsets)
            last = after(self.pending, *before)
            line = jnp.zeros((n_z,) + last.shape[1:], last.dtype)
            for i, offset in enumerate(self.offsets):
                line = place(line, self.stack[i], z_index ^ offset)
                line = place(line, last[i], z_index ^ offset ^ self.next)
            return line.reshape(-1, last.shape[2])

    class Reduce:
        def __init__(self, part):
            self.line, self.next = part.reshape(n_z, -1, part.shape[1]), 1
            self.send()

        def send(self):
            if self.next < n_z:
                bit = (z_index // self.next) % 2
                pairs = self.line.reshape((-1, 2) + self.line.shape[1:])
                self.kept = lax.dynamic_index_in_dim(pairs, bit, 1, keepdims=False)
                sent = lax.dynamic_index_in_dim(pairs, 1 - bit, 1, keepdims=False)
                self.pending = swap(sent, "z", n_z, self.next)

        def step(self, *before):
            other = after(self.pending, *before)
            self.line = (self.kept.astype(F32) + other.astype(F32)).astype(BF)
            self.next *= 2
            self.send()
            return self.line

        def finish(self, *before):
            while self.next < n_z:
                self.step(*before)
            return self.line[0]

    def gather_dp(line):
        return lax.all_gather(line, "dp", axis=0, tiled=True)

    def gather_all(shard):
        if n_dp != 4:
            full = lax.all_gather(shard, everyone, axis=0, tiled=True)
            return lambda *before: lambda *before: full
        chunk, columns = shard.shape
        line_arrive = gather_line(shard)

        def first(*before):
            line = line_arrive(*before)
            empty = jnp.zeros((n_dp, n_z, n_core, chunk, columns), shard.dtype)
            line, empty = lax.optimization_barrier((line, empty))
            near = [swap(line, "dp", n_dp, k) for k in (1, 2)]

            def second(*before):
                half = line.shape[0] // 2
                by_x, by_y = [after(v, *before) for v in near]
                far = (swap(by_y[:half], "dp", n_dp, 1), swap(by_x[half:], "dp", n_dp, 2))
                full = empty
                parts = [(line, dp, 0), (by_x, dp ^ 1, 0), (by_y, dp ^ 2, 0)]
                parts += [(far[0], dp ^ 3, 0), (far[1], dp ^ 3, n_z // 2)]
                for part, index, start in parts:
                    for held, of_core in ((part, core), (swap(part, "core", n_core, 1), 1 - core)):
                        held = held.reshape(1, -1, 1, chunk, columns)
                        full = lax.dynamic_update_slice(full, held, (index, start, of_core, 0, 0))
                return full.reshape(-1, columns)

            second.line = line
            return second

        return first

    def reduce_dp(part):
        return lax.psum_scatter(part, "dp", scatter_dimension=0, tiled=True)

    def by_core(mine, other, axis):
        first = jnp.where(core == 0, mine, other)
        second = jnp.where(core == 0, other, mine)
        return jnp.concatenate([first, second], axis=axis)

    def column_split(left, right):
        half = right.shape[1] // n_core
        mine = lax.dynamic_slice_in_dim(right, core * half, half, 1)
        other = lax.dynamic_slice_in_dim(right, (1 - core) * half, half, 1)
        both_right = jnp.concatenate([mine, swap(other, "core", n_core, 1)], axis=0)
        return both_cores(left), both_right

    def both_cores(v):
        return jnp.concatenate([v, swap(v, "core", n_core, 1)], axis=0)

    def sum_cores(v, *before):
        return v[:slots] + after(swap(v[slots:], "core", n_core, 1), *before)

    def own_rows(part):
        return by_core(*trade(part.astype(BF)), 1).astype(F32)

    def core_columns(shard):
        half = shard.shape[1] // n_core
        mine = lax.dynamic_slice_in_dim(shard, core * half, half, 1)
        other = lax.dynamic_slice_in_dim(shard, (1 - core) * half, half, 1)
        return by_core(mine, swap(other, "core", n_core, 1), 0)

    def grad_of(left, right):
        return contract(left, right, 0, 0).astype(BF)

    def trade(part):
        count = part.shape[0] // n_core
        kept = lax.dynamic_slice_in_dim(part, core * count, count, 0)
        sent = lax.dynamic_slice_in_dim(part, (1 - core) * count, count, 0)
        return kept, swap(sent, "core", n_core, 1)

    flat_text = caption.reshape(-1, caption.shape[2])
    text_left, text_right = column_split(flat_text.T, text_weight)
    def halve(v):
        count = n_dp
        while count > 1:
            count //= 2
            bit = (dp // count) % 2
            kept = lax.dynamic_slice_in_dim(v, bit * count, count, 0)
            sent = lax.dynamic_slice_in_dim(v, (1 - bit) * count, count, 0)
            v = kept + swap(sent, "dp", n_dp, count)
        return v

    def double(v, axis, n):
        k = 1
        while k < n:
            v = v + swap(v, axis, n, k)
            k *= 2
        return v

    head_rows = jnp.concatenate(
        [partial_mods, jnp.broadcast_to(own_gains, (n_dp, own_gains.shape[1]))], axis=1
    )
    head_vector = double(double(halve(after(head_rows, text_right)), "core", n_core), "z", n_z)
    mods = head_vector[:, :mods_width]
    gains = head_vector[0, mods_width:].reshape(gain_rows, WIDTH)
    shift_a, scale_a, gate_a, shift_f, scale_f, gate_f = [
        mods[:, i * WIDTH : (i + 1) * WIDTH] for i in range(6)
    ]
    gain = [gains[i : i + 1] for i in range(gain_rows)]

    own_units = down_weight.shape[0]
    unit_blocks = n_dp * n_z
    shard_rows = gate_up_weight.shape[0]
    by_units = gate_up_weight.reshape(shard_rows, 2 * unit_blocks, n_core, own_units)


    def units_of(which):
        return lax.dynamic_index_in_dim(by_units, which, 2, keepdims=False).reshape(shard_rows, -1)

    gate_up_shard = by_core(units_of(core), swap(after(units_of(1 - core), mods), "core", n_core, 1), 0)
    text_part = grad_of(text_left, text_right)
    text_sum = lax.psum_scatter(text_part, ("dp", "z"), scatter_dimension=0, tiled=True)
    joint_near = gather_all(joint_weight)(text_part)
    joint_early = getattr(joint_near, "line", text_part)
    first_shard = jnp.concatenate([gate_up_shard, core_columns(after(mixer_weight, mods))], axis=1)
    first_line = Gather(after(first_shard, joint_early))
    first_early = first_line.step()

    pad = ((0, slots - rows), (0, 0))
    xfloat = jnp.pad(tokens[0], pad).astype(F32)
    upstream = jnp.pad(cotangent[0], pad).astype(F32)
    normed_in, normed_pull = jax.vjp(modulate, xfloat, gain[0], scale_a, shift_a)
    normed_low = normed_in.astype(BF)
    joint_full = joint_near(normed_low, first_early)
    joint = product(normed_low, joint_full)
    def to_groups(parts):
        count = parts[0].shape[0]
        spread = []
        for part in parts:
            part = jnp.pad(part, ((0, 0), (0, spare * HEAD_DIM)))
            spread.append(part.reshape(count, n_seq, wide).transpose(1, 0, 2))
        return jnp.concatenate(spread, axis=2)

    def from_groups(part):
        part = part.transpose(1, 0, 2)
        return part.reshape(part.shape[0], n_seq * wide)[:, :WIDTH]

    def exchange(v):
        return lax.all_to_all(v, seq, 0, 0, tiled=True)

    lane = jnp.arange(LANES)
    freq = jnp.exp((lane % (HEAD_DIM // 2)).astype(F32) * (-jnp.log(10000.0) / (HEAD_DIM // 2)))
    angle = (seq_index * rows + jnp.arange(slots)).astype(F32)[:, None] * freq[None, :]
    cosine = jnp.cos(angle)
    sine = jnp.sin(angle) * jnp.where(lane % HEAD_DIM < HEAD_DIM // 2, -1.0, 1.0)[None, :]
    rope_gains = gains[4:6]
    half_slots = slots // 2

    def head_arrays(columns):
        return [jax.ShapeDtypeStruct((n_seq, half_slots, columns * HEAD_DIM), BF)] * heads

    def exchange_heads(arrays):
        return [exchange(v).reshape(n_seq * half_slots, -1) for v in arrays]

    def exchange_back(arrays):
        return [exchange(v.reshape(n_seq, half_slots, -1)) for v in arrays]

    sent = simple_call(group_kernel, head_arrays(6), "group_heads", joint, rope_gains, cosine, sine)
    sent = list(sent)
    first_line = first_line.finish(joint)
    sent[0] = after(sent[0], first_line)
    split_at = gate_up_shard.shape[1]
    mixer_half = gather_dp(first_line[:, split_at:])
    gate_up_half = gather_dp(first_line[:, :split_at])
    down_line = Gather(after(down_weight, first_line))
    text_raw = own_rows(after(text_sum, sent[0]))
    text_rows = text_raw.shape[0]
    text_keys, text_key_pull = jax.vjp(norm_rows, text_raw[:, :WIDTH], gain[6])
    text_own = exchange(
        to_groups([text_keys.astype(BF), text_raw[:, WIDTH:].astype(BF)])
    ).reshape(n_seq * text_rows, 2 * wide)

    sent[1] = after(sent[1], text_own)
    qkv = exchange_heads(sent)
    mixer_full = by_core(mixer_half, swap(mixer_half, "core", n_core, 1), 1)
    down_half = gather_dp(down_line.finish(qkv[0]))
    slot = jnp.arange(n_seq * slots)
    side, line = slot // (n_seq * half_slots), slot % (n_seq * half_slots)
    within = side * half_slots + line % half_slots
    shape_row = image_shape[dp]
    valid = shape_row[0] * (shape_row[1] + 1)
    live = (within < rows) & ((line // half_slots) * rows + within < valid)
    bias = jnp.where(live, 0.0, NEG).astype(BF)[:, None]
    text_bias = jnp.where(jnp.arange(TEXT) < caption_len[dp], 0.0, NEG).astype(BF)[:, None]
    tanh_gates = jnp.tanh(head_gates)
    first_head = seq_index * heads
    own_gates = lax.dynamic_slice_in_dim(jnp.pad(tanh_gates, (0, spare)), first_head, heads, 0)
    gate_rows = [jnp.broadcast_to(own_gates[i : i + 1, None], (1, HEAD_DIM)) for i in range(heads)]
    attended = [
        attend_forward(qkv[i], text_own, bias, text_bias, gate_rows[i], i, 2 * half_slots)
        for i in range(heads)
    ]
    token_shape = jax.ShapeDtypeStruct((slots, WIDTH), BF)
    mixed = simple_call(
        join_kernel, token_shape, "join_heads", *exchange_back([v[0] for v in attended])
    )
    proj = product(mixed, mixer_full)
    branch_a, branch_a_pull = jax.vjp(branch_out, proj, gain[1], gate_a)
    hstate = xfloat + branch_a
    ffn_in, ffn_in_pull = jax.vjp(modulate, hstate, gain[2], scale_f, shift_f)

    ffn_both = both_cores(ffn_in.astype(BF))
    gate_up = product(ffn_both, gate_up_half)
    hidden, swiglu_pull = jax.vjp(swiglu, gate_up)
    hidden_low = hidden.astype(BF)
    ffn = sum_cores(product(hidden_low, down_half))
    branch_f, branch_f_pull = jax.vjp(branch_out, ffn, gain[3], gate_f)
    output = (hstate + branch_f).astype(BF)[None, :rows]

    ffn_grad, gain3_grad, gate_f_grad = branch_f_pull(upstream)
    ffn_grad_both = both_cores(ffn_grad.astype(BF))
    (gate_up_grad_rows,) = swiglu_pull(contract(ffn_grad_both, down_half, 1, 1))
    gate_up_low = gate_up_grad_rows.astype(BF)
    down_part = grad_of(hidden_low, ffn_grad_both)
    gate_up_part = grad_of(ffn_both, after(gate_up_low, down_part))
    down_part = reduce_dp(down_part)
    state_part, gain2_grad, scale_f_grad, shift_f_grad = ffn_in_pull(
        sum_cores(contract(gate_up_low, gate_up_half, 1, 1), gate_up_part)
    )
    state_grad = upstream + state_part
    proj_grad, gain1_grad, gate_a_grad = branch_a_pull(state_grad)
    proj_low = proj_grad.astype(BF)
    mixed_grad = contract(proj_low, mixer_full, 1, 1).astype(BF)
    ups = exchange_heads(simple_call(split_kernel, head_arrays(2), "split_heads", mixed_grad))
    mixer_part = grad_of(*column_split(mixed, after(proj_low, mixed_grad)))
    ups[0] = after(ups[0], mixer_part)
    gate_up_part = reduce_dp(after(gate_up_part, mixer_part))
    mixer_part = reduce_dp(mixer_part)
    ups[-1] = after(ups[-1], down_part)
    grads, dtexts, dgates = zip(*[
        attend_backward(
            qkv[i], text_own, bias, text_bias, gate_rows[i], ups[i], *attended[i][1:], i, 2 * half_slots
        )
        for i in range(heads)
    ])
    grads = list(grads)
    down_sum = Reduce(down_part)
    grads[0] = after(grads[0], down_sum.step())
    down_out = down_sum.finish()
    grads[-2] = after(grads[-2], down_out)
    down_out = down_out.astype(F32)
    grouped = exchange_back(grads)
    joint_low, rope_gain_grads = simple_call(
        functools.partial(ungroup_kernel, heads),
        [jax.ShapeDtypeStruct((slots, 3 * WIDTH), BF), jax.ShapeDtypeStruct((2, WIDTH), F32)],
        "ungroup_heads", *grouped, joint, rope_gains, cosine, sine,
    )
    joint_left, joint_right = column_split(normed_low, joint_low)
    piece = joint_right.shape[1] // 2
    joint_parts = [grad_of(joint_left, joint_right[:, p * piece : (p + 1) * piece]) for p in range(2)]
    joint_parts = [reduce_dp(after(part, gate_up_part, mixer_part)) for part in joint_parts]
    gate_up_sum = Reduce(gate_up_part)
    later_low = after(joint_low, gate_up_sum.step(joint_low))
    input_part, gain0_grad, scale_a_grad, shift_a_grad = normed_pull(
        contract(later_low, joint_full, 1, 1)
    )
    tokens_grad = (state_grad + input_part).astype(BF)[None, :rows]
    dtext = jnp.concatenate([v[:, :HEAD_DIM] for v in dtexts] + [v[:, HEAD_DIM:] for v in dtexts], axis=1)
    text_back = exchange(dtext.reshape(n_seq, text_rows, 2 * wide))
    text_key_grad, gain6_grad = text_key_pull(from_groups(text_back[:, :, :wide]).astype(F32))
    text_grad_rows = jnp.concatenate(
        [text_key_grad.astype(BF), from_groups(text_back[:, :, wide:])], axis=1
    )
    text_grad_all = lax.all_gather(after(text_grad_rows, joint_low), everyone, axis=0, tiled=True)
    text_grad = contract(flat_text, after(text_grad_all, joint_parts[1]), 0, 0)

    gates_own = jnp.concatenate([jnp.sum(v, axis=1) for v in dgates]) * (1.0 - own_gates * own_gates)
    gates_all = lax.dynamic_update_slice_in_dim(jnp.zeros((WIDTH,), F32), gates_own, first_head, 0)[None, :]
    pieces = [shift_a_grad, scale_a_grad, gate_a_grad, shift_f_grad, scale_f_grad, gate_f_grad]
    shared = [
        gain0_grad, gain1_grad, gain2_grad, gain3_grad, rope_gain_grads[0:1], rope_gain_grads[1:2], gain6_grad,
    ]
    tail = pieces + shared + [gates_all]
    tail = simple_call(
        pack_kernel, jax.ShapeDtypeStruct((-(-len(tail) // 8) * 8, WIDTH), F32), "pack_rows", *tail
    )
    gate_up_sum = gate_up_sum.finish(tail)
    joint_sums = [Reduce(after(part, tail)) for part in joint_parts]
    tails = [after(double(double(tail, "core", n_core), "z", n_z), gate_up_sum, joint_sums[0].step())]
    kept, received = [
        v.reshape(shard_rows, 2 * unit_blocks, 1, own_units)
        for v in trade(gate_up_sum)
    ]
    gate_up_out = by_core(kept, received, 2).reshape(shard_rows, -1).astype(F32)
    joint_sums = [part.finish(tails[0]) for part in joint_sums]
    joint_out = own_rows(jnp.concatenate(joint_sums, axis=1))
    mixer_out = own_rows(Reduce(after(mixer_part, tails[0])).finish())
    while len(tails) < n_dp:
        tails += list(swap(jnp.stack(tails), "dp", n_dp, len(tails)))
    count = len(pieces)
    total = tree([t[count:] for t in tails])
    gates_grad = total[gain_rows, :HEADS]
    gains_grad = lax.dynamic_slice_in_dim(total[:gain_rows], device * gain_width, gain_width, 1)
    mods_low = jnp.stack([t[:count].astype(BF).reshape(-1) for t in tails])
    cond_rows = jnp.concatenate(
        [lax.dynamic_slice_in_dim(soft_cond, dp ^ k, 1, 0) for k in range(n_dp)], axis=0
    )
    modulation_grad = contract(cond_rows, mods_low, 0, 0)
    bias_grad = lax.dynamic_slice_in_dim(
        jnp.sum(mods_low.astype(F32), axis=0), bias_start, bias_width, 0
    )
    return (
        output,
        tokens_grad,
        joint_out,
        mixer_out,
        gate_up_out,
        down_out,
        text_grad,
        modulation_grad,
        bias_grad,
        gains_grad,
        gates_grad,
    )


def solution(mesh):
    n_dp, n_seq = mesh.shape["dp"], mesh.shape["seq"]
    sizes = (n_dp, n_seq // 2, 2)
    split = Mesh(mesh.devices.reshape(sizes), ("dp", "z", "core"))
    seq, everyone = ("z", "core"), ("dp", "z", "core")
    token_spec, row_spec, column_spec = P("dp", seq, None), P(everyone, None), P(None, everyone)
    in_specs = (
        token_spec, column_spec, P(None, None, everyone), P(), P(), token_spec,
        row_spec, row_spec, row_spec, row_spec, row_spec, row_spec, P(everyone), column_spec, P(),
    )
    out_specs = (
        token_spec, token_spec, row_spec, row_spec, row_spec, row_spec, row_spec, row_spec,
        P(everyone), column_spec, P(),
    )
    return jax.shard_map(
        functools.partial(local, sizes), mesh=split, in_specs=in_specs, out_specs=out_specs, check_vma=False
    )
```

```python
import functools

import jax
import jax.numpy as jnp
from jax import lax
from jax.experimental import pallas as pl
from jax.experimental.pallas import tpu as pltpu
from jax.sharding import Mesh
from jax.sharding import PartitionSpec as P

HEADS = 24
HEAD_DIM = 64
TEXT = 256
WIDTH = HEADS * HEAD_DIM
EPS = 1e-06
NEG = -1e30
SCALE = float(HEAD_DIM) ** (-0.5)
LANES = 128
BF = jnp.bfloat16
F32 = jnp.float32
VMEM_BYTES = 56 << 20


def norm_rows(v, gain):
    return v * lax.rsqrt(jnp.mean(v * v, axis=-1, keepdims=True) + EPS) * gain


def modulate(v, gain, scale, shift):
    return norm_rows(v, gain) * (1.0 + scale) + shift


def branch_out(v, gain, gate):
    return gate * norm_rows(v, gain)


def swiglu(gate_up):
    half = gate_up.shape[-1] // 2
    return jax.nn.silu(gate_up[:, :half]) * gate_up[:, half:]


def product(left, right):
    return jnp.dot(left, right, preferred_element_type=F32)


def contract(left, right, left_dim, right_dim):
    return lax.dot_general(
        left, right, (((left_dim,), (right_dim,)), ((), ())), preferred_element_type=F32
    )


def split3(v):
    high = v.astype(BF)
    rest = v - high.astype(F32)
    mid = rest.astype(BF)
    return [high, mid, (rest - mid.astype(F32)).astype(BF)]


def extend(block, columns):
    rows = block.shape[0]
    fill = HEAD_DIM - len(columns)
    return jnp.concatenate([block] + list(columns) + [jnp.zeros((rows, fill), BF)], axis=1)


def unfold(v, start, period):
    return jnp.concatenate(
        [v[:, start : start + HEAD_DIM], v[:, period + start : period + start + HEAD_DIM]], axis=0
    )


def fold(parts):
    rows = parts[0].shape[0] // 2
    return jnp.concatenate([p[:rows] for p in parts] + [p[rows:] for p in parts], axis=1)


def spread_keys(index, qkv_ref, text_ref, bias_ref, text_bias_ref, outs, key_ones, value_ones):
    wide = text_ref.shape[1] // 2
    at = index * HEAD_DIM
    sources = (
        (unfold(qkv_ref, HEAD_DIM, 3 * HEAD_DIM), unfold(qkv_ref, 2 * HEAD_DIM, 3 * HEAD_DIM), bias_ref),
        (text_ref[:, at : at + HEAD_DIM], text_ref[:, wide + at : wide + at + HEAD_DIM], text_bias_ref),
    )
    for i, (keys, values, bias) in enumerate(sources):
        one = jnp.ones((keys.shape[0], 1), BF)
        outs[2 * i][...] = extend(keys, [bias[...]] + [one] * key_ones)
        outs[2 * i + 1][...] = extend(values, [one] * value_ones)


def attend_forward_kernel(
    index, qkv_ref, text_ref, bias_ref, text_bias_ref, gate_ref, q_ref,
    mixed_ref, own_ref, cross_ref, lse_ref, *spread
):
    @pl.when(pl.program_id(0) == 0)
    def _():
        spread_keys(index, qkv_ref, text_ref, bias_ref, text_bias_ref, spread, 0, 1)

    query = unfold(q_ref, 0, 3 * HEAD_DIM) * SCALE
    query = extend(query, [jnp.ones((query.shape[0], 1), BF)])

    def soft(keys, values):
        scores = contract(query, keys[...], 1, 1)
        high = jnp.max(scores, axis=1, keepdims=True)
        total = contract(jnp.exp(scores - high).astype(BF), values[...], 1, 0)
        mass = total[:, HEAD_DIM : HEAD_DIM + 1]
        return total[:, :HEAD_DIM] / mass, high + jnp.log(mass)

    own, own_lse = soft(spread[0], spread[1])
    cross, cross_lse = soft(spread[2], spread[3])
    own_ref[...] = fold([own])
    cross_ref[...] = fold([cross])
    mixed_ref[...] = fold([own + gate_ref[...] * cross]).astype(BF)
    lse_ref[...] = fold([own_lse, cross_lse])


def attend_backward_kernel(
    index, qkv_ref, text_ref, bias_ref, text_bias_ref, gate_ref, q_ref, up_ref, own_ref, cross_ref, lse_ref,
    grad_ref, dtext_ref, dgate_ref, *scratch
):
    spread, sums = scratch[:4], scratch[4:]
    step = pl.program_id(0)

    @pl.when(step == 0)
    def _():
        spread_keys(index, qkv_ref, text_ref, bias_ref, text_bias_ref, spread, 3, 3)
        for ref in sums + (dgate_ref,):
            ref[...] = jnp.zeros_like(ref)

    query = unfold(q_ref, 0, 3 * HEAD_DIM)
    one = jnp.ones((query.shape[0], 1), BF)
    up = unfold(up_ref, 0, HEAD_DIM)
    cross = unfold(cross_ref, 0, HEAD_DIM)
    up_float = up.astype(F32)
    up_cross = (gate_ref[...] * up_float).astype(BF)
    dgate_ref[...] += jnp.sum(up_float * cross, axis=0, keepdims=True)
    half = lse_ref.shape[0]
    lse = jnp.concatenate([lse_ref[:, 0:2], lse_ref[:, 2:4]], axis=0)

    def one_soft(upstream, row, spread_lse, keys, values, key_sum, value_sum):
        center = jnp.sum(row, axis=1, keepdims=True)
        left = extend(query * SCALE, [one] + [-part for part in split3(spread_lse)])
        weights = jnp.exp(contract(left, keys[...], 1, 1))
        left = extend(upstream, [-part for part in split3(center)])
        score_grad = (weights * contract(left, values[...], 1, 1)).astype(BF)
        weights = weights.astype(BF)
        key_sum[...] += contract(score_grad, query, 0, 0)
        value_sum[...] += contract(weights, upstream, 0, 0)
        return contract(score_grad, keys[...], 1, 0)[:, :HEAD_DIM]

    dq = one_soft(
        up, up_float * unfold(own_ref, 0, HEAD_DIM), lse[:, 0:1], spread[0], spread[1], sums[0], sums[1]
    )
    dq += one_soft(
        up_cross, up_cross.astype(F32) * cross, lse[:, 1:2], spread[2], spread[3], sums[2], sums[3]
    )
    dq = (dq * SCALE).astype(BF)
    here = pl.ds(pl.multiple_of(step * half, half), half)
    grad_ref[here, 0:HEAD_DIM] = dq[:half]
    grad_ref[here, 3 * HEAD_DIM : 4 * HEAD_DIM] = dq[half:]

    @pl.when(step == pl.num_programs(0) - 1)
    def _():
        slots = grad_ref.shape[0]
        both = jnp.concatenate([sums[0][...] * SCALE, sums[1][...]], axis=1).astype(BF)
        grad_ref[:, HEAD_DIM : 3 * HEAD_DIM] = both[:slots]
        grad_ref[:, 4 * HEAD_DIM :] = both[slots:]
        dtext_ref[...] = jnp.concatenate([sums[2][...] * SCALE, sums[3][...]], axis=1).astype(BF)


def whole_block(shape):
    return pl.BlockSpec(shape, lambda i: (0,) * len(shape), pipeline_mode=pl.Buffered(1))


def row_block(rows, columns):
    return pl.BlockSpec((rows, columns), lambda i: (i, 0))


def params():
    return pltpu.CompilerParams(vmem_limit_bytes=VMEM_BYTES)


def cost(flops, size, exps=0):
    return pl.CostEstimate(flops=int(flops), bytes_accessed=int(size), transcendentals=int(exps))


def attend_forward(qkv, text, bias, text_bias, gate, index, rows):
    half, words, head = qkv.shape[0], text.shape[0], HEAD_DIM
    slots = 2 * half
    pairs = slots * (slots + words)
    return pl.pallas_call(
        functools.partial(attend_forward_kernel, index),
        grid=(half // rows,),
        in_specs=[
            whole_block((half, 6 * head)), whole_block(text.shape), whole_block((slots, 1)),
            whole_block((words, 1)), whole_block((1, head)), row_block(rows, 6 * head),
        ],
        out_specs=[row_block(rows, 2 * head)] * 3 + [row_block(rows, 4)],
        out_shape=[
            jax.ShapeDtypeStruct((half, 2 * head), BF),
            jax.ShapeDtypeStruct((half, 2 * head), F32),
            jax.ShapeDtypeStruct((half, 2 * head), F32),
            jax.ShapeDtypeStruct((half, 4), F32),
        ],
        scratch_shapes=[pltpu.VMEM((n, 2 * head), BF) for n in (slots, slots, words, words)],
        compiler_params=params(),
        cost_estimate=cost(pairs * head * 16, slots * head * 18, pairs),
        name="attend_forward",
    )(qkv, text, bias, text_bias, gate, qkv)


def attend_backward(qkv, text, bias, text_bias, gate, up, own, cross, lse, index, rows):
    half, words, head = qkv.shape[0], text.shape[0], HEAD_DIM
    slots = 2 * half
    pairs = slots * (slots + words)
    return pl.pallas_call(
        functools.partial(attend_backward_kernel, index),
        grid=(half // rows,),
        in_specs=[
            whole_block((half, 6 * head)), whole_block(text.shape), whole_block((slots, 1)),
            whole_block((words, 1)), whole_block((1, head)), row_block(rows, 6 * head),
            row_block(rows, 2 * head), row_block(rows, 2 * head), row_block(rows, 2 * head), row_block(rows, 4),
        ],
        out_specs=[whole_block((half, 6 * head)), whole_block((words, 2 * head)), whole_block((1, head))],
        out_shape=[
            jax.ShapeDtypeStruct((half, 6 * head), BF),
            jax.ShapeDtypeStruct((words, 2 * head), BF),
            jax.ShapeDtypeStruct((1, head), F32),
        ],
        scratch_shapes=[pltpu.VMEM((n, 2 * head), BF) for n in (slots, slots, words, words)]
        + [pltpu.VMEM((n, head), F32) for n in (slots, slots, words, words)],
        compiler_params=params(),
        cost_estimate=cost(pairs * head * 40, slots * head * 26, pairs),
        name="attend_backward",
    )(qkv, text, bias, text_bias, gate, qkv, up, own, cross, lse)


def swap_halves(v):
    lane = lax.broadcasted_iota(jnp.int32, v.shape, 1)
    half = HEAD_DIM // 2
    return jnp.where(
        lane % HEAD_DIM < half, pltpu.roll(v, LANES - half, 1), pltpu.roll(v, half, 1)
    )


def tiles_of(v):
    return [v[:, t : t + LANES] for t in range(0, v.shape[1], LANES)]


def split_heads(parts, out_refs):
    heads, groups = len(out_refs), out_refs[0].shape[0]
    rows = parts[0].shape[0]
    for g in range(groups):
        for i in range(heads):
            at = (g * heads + i) * HEAD_DIM
            if at < WIDTH:
                out_refs[i][g] = fold([part[:, at : at + HEAD_DIM] for part in parts])
            else:
                out_refs[i][g] = jnp.zeros(out_refs[i].shape[1:], out_refs[i].dtype)


def join_heads(refs, which, count):
    groups, columns = refs[0].shape[0], []
    for g in range(groups):
        for i, ref in enumerate(refs):
            if (g * len(refs) + i) * HEAD_DIM < WIDTH:
                columns.append(unfold(ref.at[g], which * HEAD_DIM, count * HEAD_DIM))
    return jnp.concatenate(columns, axis=1)


def group_kernel(joint_ref, gains_ref, cos_ref, sin_ref, *out_refs):
    cosine, sine = cos_ref[...], sin_ref[...]
    parts = []
    for which in range(2):
        raw = joint_ref[:, which * WIDTH : (which + 1) * WIDTH]
        root = lax.rsqrt(jnp.mean(raw * raw, axis=1, keepdims=True) + EPS)
        scaled = raw * root * gains_ref[which : which + 1, :]
        turned = [tile * cosine + swap_halves(tile) * sine for tile in tiles_of(scaled)]
        parts.append(jnp.concatenate(turned, axis=1).astype(BF))
    parts.append(joint_ref[:, 2 * WIDTH :].astype(BF))
    split_heads(parts, out_refs)


def ungroup_kernel(heads, *refs):
    grad_refs = refs[:heads]
    joint_ref, gains_ref, cos_ref, sin_ref, out_ref, dgain_ref = refs[heads:]
    cosine, sine = cos_ref[...], sin_ref[...]
    for which in range(2):
        cut = slice(which * WIDTH, (which + 1) * WIDTH)
        grad = join_heads(grad_refs, which, 3).astype(F32)
        turned = [tile * cosine - swap_halves(tile) * sine for tile in tiles_of(grad)]
        grad = jnp.concatenate(turned, axis=1)
        raw = joint_ref[:, cut]
        root = lax.rsqrt(jnp.mean(raw * raw, axis=1, keepdims=True) + EPS)
        unit = raw * root
        dgain_ref[which : which + 1, :] = jnp.sum(grad * unit, axis=0, keepdims=True)
        grad = grad * gains_ref[which : which + 1, :]
        grad = root * (grad - unit * jnp.mean(grad * unit, axis=1, keepdims=True))
        out_ref[:, cut] = grad.astype(BF)
    out_ref[:, 2 * WIDTH :] = join_heads(grad_refs, 2, 3)


def split_kernel(value_ref, *out_refs):
    split_heads([value_ref[...]], out_refs)


def join_kernel(*refs):
    refs[-1][...] = join_heads(refs[:-1], 0, 1)


def swiglu_back_kernel(grad_ref, weight_ref, gate_ref, up_ref, out_ref):
    size, half = gate_ref.shape[1], out_ref.shape[1] // 2
    grad = contract(grad_ref[...], weight_ref[...], 1, 1)
    gate = gate_ref[...]
    sig = jax.nn.sigmoid(gate)
    at = pl.multiple_of(pl.program_id(0) * size, size)
    out_ref[:, pl.ds(at, size)] = (grad * up_ref[...] * (sig * (1.0 + gate * (1.0 - sig)))).astype(BF)
    out_ref[:, pl.ds(half + at, size)] = (grad * (gate * sig)).astype(BF)


def swiglu_back(grad, weight, gate_up):
    rows, width = grad.shape
    units = weight.shape[0]
    size = 2 * LANES
    count = units // size
    return pl.pallas_call(
        swiglu_back_kernel,
        grid=(count,),
        in_specs=[
            whole_block((rows, width)), row_block(size, width),
            pl.BlockSpec((rows, size), lambda i: (0, i)), pl.BlockSpec((rows, size), lambda i: (0, count + i)),
        ],
        out_specs=whole_block((rows, 2 * units)),
        out_shape=jax.ShapeDtypeStruct((rows, 2 * units), BF),
        compiler_params=params(),
        cost_estimate=cost(2 * rows * width * units, rows * units * 12 + units * width * 2, rows * units),
        name="swiglu_back",
    )(grad, weight, gate_up, gate_up)


def pack_kernel(*refs):
    out_ref = refs[-1]
    rows = [ref[...] for ref in refs[:-1]]
    rows.append(jnp.zeros((out_ref.shape[0] - len(rows), out_ref.shape[1]), F32))
    out_ref[...] = jnp.concatenate(rows, axis=0)


def simple_call(kernel, out_shape, name, *args):
    size = sum(a.size * a.dtype.itemsize for a in args)
    shapes = out_shape if isinstance(out_shape, list) else [out_shape]
    return pl.pallas_call(
        kernel,
        in_specs=[pl.BlockSpec(memory_space=pltpu.VMEM)] * len(args),
        out_specs=jax.tree.map(lambda _: pl.BlockSpec(memory_space=pltpu.VMEM), out_shape),
        out_shape=out_shape,
        compiler_params=params(),
        cost_estimate=cost(size * 8, size + sum(o.size * o.dtype.itemsize for o in shapes)),
        name=name,
    )(*args)


def local(
    sizes,
    tokens,
    condition,
    caption,
    caption_len,
    image_shape,
    cotangent,
    joint_weight,
    mixer_weight,
    gate_up_weight,
    down_weight,
    text_weight,
    modulation_weight,
    modulation_bias,
    norm_gains,
    head_gates,
):
    n_dp, n_z, n_core = sizes
    everyone = ("dp", "z", "core")
    seq = ("z", "core")
    n_seq = n_z * n_core
    heads = -(-HEADS // n_seq)
    wide = heads * HEAD_DIM
    spare = n_seq * heads - HEADS
    rows = tokens.shape[1]
    slots = -(-rows // 16) * 16
    dp = lax.axis_index("dp")
    core = lax.axis_index("core")
    z_index = lax.axis_index("z")
    seq_index = lax.axis_index(seq)
    device = lax.axis_index(everyone)

    def swap(v, axis, n, k):
        return lax.ppermute(v, axis, [(i, i ^ k) for i in range(n)])

    def tree(parts):
        while len(parts) > 1:
            parts = [parts[i] + parts[i + 1] for i in range(0, len(parts), 2)]
        return parts[0]

    def sum_over(v, axis, n):
        return tree([v] + [swap(v, axis, n, k) for k in range(1, n)])

    soft_cond = jax.nn.silu(condition).astype(BF)
    partial_mods = product(soft_cond, modulation_weight)
    bias_width = modulation_bias.shape[0]
    bias_start = device * bias_width
    with_bias = (
        lax.dynamic_slice_in_dim(partial_mods, bias_start, bias_width, 1) + modulation_bias[None, :]
    )
    partial_mods = lax.dynamic_update_slice_in_dim(partial_mods, with_bias, bias_start, 1)
    mods_width = partial_mods.shape[1]
    gain_rows, gain_width = norm_gains.shape
    own_gains = lax.dynamic_update_slice_in_dim(
        jnp.zeros((gain_rows, WIDTH), F32), norm_gains.astype(F32), device * gain_width, 1
    ).reshape(1, -1)

    def after(v, *others):
        return lax.optimization_barrier((v,) + others)[0]

    def shift_z(v, k):
        return lax.ppermute(v, "z", [(i, (i + k) % n_z) for i in range(n_z)])

    def place(full, part, index):
        return lax.dynamic_update_slice(full, part[None], (index,) + (0,) * part.ndim)


    def gather_line(shard):
        parts = [shift_z(shard, k) for k in range(1, n_z)]

        def arrive(*before):
            line = place(jnp.zeros((n_z,) + shard.shape, shard.dtype), shard, z_index)
            for k, part in enumerate(parts, 1):
                line = place(line, after(part, *before), (z_index - k) % n_z)
            return line.reshape(-1, shard.shape[1])

        return arrive

    class Gather:
        def __init__(self, shard):
            self.stack, self.offsets, self.next = shard[None], [0], n_z // 2
            self.send()

        def send(self):
            self.pending = swap(self.stack, "z", n_z, self.next) if self.next else None

        def step(self, *before):
            other = after(self.pending, *before)
            self.offsets = self.offsets + [offset ^ self.next for offset in self.offsets]
            self.stack = jnp.concatenate([self.stack, other], axis=0)
            self.next //= 2
            self.send()
            return self.stack

        def finish(self, *before):
            while self.next > 1:
                self.step(*before)
            count = len(self.offsets)
            last = after(self.pending, *before)
            line = jnp.zeros((n_z,) + last.shape[1:], last.dtype)
            for i, offset in enumerate(self.offsets):
                line = place(line, self.stack[i], z_index ^ offset)
                line = place(line, last[i], z_index ^ offset ^ self.next)
            return line.reshape(-1, last.shape[2])

    class Reduce:
        def __init__(self, part):
            self.line, self.next = part.reshape(n_z, -1, part.shape[1]), 1
            self.send()

        def send(self):
            if self.next < n_z:
                bit = (z_index // self.next) % 2
                pairs = self.line.reshape((-1, 2) + self.line.shape[1:])
                self.kept = lax.dynamic_index_in_dim(pairs, bit, 1, keepdims=False)
                sent = lax.dynamic_index_in_dim(pairs, 1 - bit, 1, keepdims=False)
                self.pending = swap(sent, "z", n_z, self.next)

        def step(self, *before):
            other = after(self.pending, *before)
            self.line = (self.kept.astype(F32) + other.astype(F32)).astype(BF)
            self.next *= 2
            self.send()
            return self.line

        def finish(self, *before):
            while self.next < n_z:
                self.step(*before)
            return self.line[0]

    def gather_dp(line):
        return lax.all_gather(line, "dp", axis=0, tiled=True)

    def gather_all(shard):
        if n_dp != 4:
            full = lax.all_gather(shard, everyone, axis=0, tiled=True)
            return lambda *before: lambda *before: full
        chunk, columns = shard.shape
        line_arrive = gather_line(shard)

        def first(*before):
            line = line_arrive(*before)
            empty = jnp.zeros((n_dp, n_z, n_core, chunk, columns), shard.dtype)
            line, empty = lax.optimization_barrier((line, empty))
            near = [swap(line, "dp", n_dp, k) for k in (1, 2)]

            def second(*before):
                half = line.shape[0] // 2
                by_x, by_y = [after(v, *before) for v in near]
                far = (swap(by_y[:half], "dp", n_dp, 1), swap(by_x[half:], "dp", n_dp, 2))
                full = empty
                parts = [(line, dp, 0), (by_x, dp ^ 1, 0), (by_y, dp ^ 2, 0)]
                parts += [(far[0], dp ^ 3, 0), (far[1], dp ^ 3, n_z // 2)]
                for part, index, start in parts:
                    for held, of_core in ((part, core), (swap(part, "core", n_core, 1), 1 - core)):
                        held = held.reshape(1, -1, 1, chunk, columns)
                        full = lax.dynamic_update_slice(full, held, (index, start, of_core, 0, 0))
                return full.reshape(-1, columns)

            second.line = line
            return second

        return first

    def reduce_dp(part):
        return lax.psum_scatter(part, "dp", scatter_dimension=0, tiled=True)

    def by_core(mine, other, axis):
        first = jnp.where(core == 0, mine, other)
        second = jnp.where(core == 0, other, mine)
        return jnp.concatenate([first, second], axis=axis)

    def column_split(left, right):
        half = right.shape[1] // n_core
        mine = lax.dynamic_slice_in_dim(right, core * half, half, 1)
        other = lax.dynamic_slice_in_dim(right, (1 - core) * half, half, 1)
        both_right = jnp.concatenate([mine, swap(other, "core", n_core, 1)], axis=0)
        return both_cores(left), both_right

    def both_cores(v):
        return jnp.concatenate([v, swap(v, "core", n_core, 1)], axis=0)

    def sum_cores(v, *before):
        return v[:slots] + after(swap(v[slots:], "core", n_core, 1), *before)

    def own_rows(part):
        return by_core(*trade(part.astype(BF)), 1).astype(F32)

    def core_columns(shard):
        half = shard.shape[1] // n_core
        mine = lax.dynamic_slice_in_dim(shard, core * half, half, 1)
        other = lax.dynamic_slice_in_dim(shard, (1 - core) * half, half, 1)
        return by_core(mine, swap(other, "core", n_core, 1), 0)

    def grad_of(left, right):
        return contract(left, right, 0, 0).astype(BF)

    def trade(part):
        count = part.shape[0] // n_core
        kept = lax.dynamic_slice_in_dim(part, core * count, count, 0)
        sent = lax.dynamic_slice_in_dim(part, (1 - core) * count, count, 0)
        return kept, swap(sent, "core", n_core, 1)

    flat_text = caption.reshape(-1, caption.shape[2])
    text_left, text_right = column_split(flat_text.T, text_weight)
    def halve(v):
        count = n_dp
        while count > 1:
            count //= 2
            bit = (dp // count) % 2
            kept = lax.dynamic_slice_in_dim(v, bit * count, count, 0)
            sent = lax.dynamic_slice_in_dim(v, (1 - bit) * count, count, 0)
            v = kept + swap(sent, "dp", n_dp, count)
        return v

    def double(v, axis, n):
        k = 1
        while k < n:
            v = v + swap(v, axis, n, k)
            k *= 2
        return v

    head_rows = jnp.concatenate(
        [partial_mods, jnp.broadcast_to(own_gains, (n_dp, own_gains.shape[1]))], axis=1
    )
    head_vector = double(double(halve(after(head_rows, text_right)), "core", n_core), "z", n_z)
    mods = head_vector[:, :mods_width]
    gains = head_vector[0, mods_width:].reshape(gain_rows, WIDTH)
    shift_a, scale_a, gate_a, shift_f, scale_f, gate_f = [
        mods[:, i * WIDTH : (i + 1) * WIDTH] for i in range(6)
    ]
    gain = [gains[i : i + 1] for i in range(gain_rows)]

    own_units = down_weight.shape[0]
    unit_blocks = n_dp * n_z
    shard_rows = gate_up_weight.shape[0]
    by_units = gate_up_weight.reshape(shard_rows, 2 * unit_blocks, n_core, own_units)


    def units_of(which):
        return lax.dynamic_index_in_dim(by_units, which, 2, keepdims=False).reshape(shard_rows, -1)

    gate_up_shard = by_core(units_of(core), swap(after(units_of(1 - core), mods), "core", n_core, 1), 0)
    text_part = grad_of(text_left, text_right)
    text_sum = lax.psum_scatter(text_part, ("dp", "z"), scatter_dimension=0, tiled=True)
    joint_near = gather_all(joint_weight)(text_part)
    joint_early = getattr(joint_near, "line", text_part)
    first_shard = jnp.concatenate([gate_up_shard, core_columns(after(mixer_weight, mods))], axis=1)
    first_line = Gather(after(first_shard, joint_early))
    first_early = first_line.step()

    pad = ((0, slots - rows), (0, 0))
    xfloat = jnp.pad(tokens[0], pad).astype(F32)
    upstream = jnp.pad(cotangent[0], pad).astype(F32)
    normed_in, normed_pull = jax.vjp(modulate, xfloat, gain[0], scale_a, shift_a)
    normed_low = normed_in.astype(BF)
    joint_full = joint_near(normed_low, first_early)
    joint = product(normed_low, joint_full)
    def to_groups(parts):
        count = parts[0].shape[0]
        spread = []
        for part in parts:
            part = jnp.pad(part, ((0, 0), (0, spare * HEAD_DIM)))
            spread.append(part.reshape(count, n_seq, wide).transpose(1, 0, 2))
        return jnp.concatenate(spread, axis=2)

    def from_groups(part):
        part = part.transpose(1, 0, 2)
        return part.reshape(part.shape[0], n_seq * wide)[:, :WIDTH]

    def exchange(v):
        return lax.all_to_all(v, seq, 0, 0, tiled=True)

    lane = jnp.arange(LANES)
    freq = jnp.exp((lane % (HEAD_DIM // 2)).astype(F32) * (-jnp.log(10000.0) / (HEAD_DIM // 2)))
    angle = (seq_index * rows + jnp.arange(slots)).astype(F32)[:, None] * freq[None, :]
    cosine = jnp.cos(angle)
    sine = jnp.sin(angle) * jnp.where(lane % HEAD_DIM < HEAD_DIM // 2, -1.0, 1.0)[None, :]
    rope_gains = gains[4:6]
    half_slots = slots // 2

    def head_arrays(columns):
        return [jax.ShapeDtypeStruct((n_seq, half_slots, columns * HEAD_DIM), BF)] * heads

    def exchange_heads(arrays):
        return [exchange(v).reshape(n_seq * half_slots, -1) for v in arrays]

    def exchange_back(arrays):
        return [exchange(v.reshape(n_seq, half_slots, -1)) for v in arrays]

    sent = simple_call(group_kernel, head_arrays(6), "group_heads", joint, rope_gains, cosine, sine)
    sent = list(sent)
    first_line = first_line.finish(joint)
    sent[0] = after(sent[0], first_line)
    split_at = gate_up_shard.shape[1]
    mixer_half = gather_dp(first_line[:, split_at:])
    gate_up_half = gather_dp(first_line[:, :split_at])
    down_line = Gather(after(down_weight, first_line))
    text_raw = own_rows(after(text_sum, sent[0]))
    text_rows = text_raw.shape[0]
    text_keys, text_key_pull = jax.vjp(norm_rows, text_raw[:, :WIDTH], gain[6])
    text_own = exchange(
        to_groups([text_keys.astype(BF), text_raw[:, WIDTH:].astype(BF)])
    ).reshape(n_seq * text_rows, 2 * wide)

    sent[1] = after(sent[1], text_own)
    qkv = exchange_heads(sent)
    mixer_full = by_core(mixer_half, swap(mixer_half, "core", n_core, 1), 1)
    down_half = gather_dp(down_line.finish(qkv[0]))
    slot = jnp.arange(n_seq * slots)
    side, line = slot // (n_seq * half_slots), slot % (n_seq * half_slots)
    within = side * half_slots + line % half_slots
    shape_row = image_shape[dp]
    valid = shape_row[0] * (shape_row[1] + 1)
    live = (within < rows) & ((line // half_slots) * rows + within < valid)
    bias = jnp.where(live, 0.0, NEG).astype(BF)[:, None]
    text_bias = jnp.where(jnp.arange(TEXT) < caption_len[dp], 0.0, NEG).astype(BF)[:, None]
    tanh_gates = jnp.tanh(head_gates)
    first_head = seq_index * heads
    own_gates = lax.dynamic_slice_in_dim(jnp.pad(tanh_gates, (0, spare)), first_head, heads, 0)
    gate_rows = [jnp.broadcast_to(own_gates[i : i + 1, None], (1, HEAD_DIM)) for i in range(heads)]
    attended = [
        attend_forward(qkv[i], text_own, bias, text_bias, gate_rows[i], i, 4 * half_slots)
        for i in range(heads)
    ]
    token_shape = jax.ShapeDtypeStruct((slots, WIDTH), BF)
    mixed = simple_call(
        join_kernel, token_shape, "join_heads", *exchange_back([v[0] for v in attended])
    )
    proj = product(mixed, mixer_full)
    branch_a, branch_a_pull = jax.vjp(branch_out, proj, gain[1], gate_a)
    hstate = xfloat + branch_a
    ffn_in, ffn_in_pull = jax.vjp(modulate, hstate, gain[2], scale_f, shift_f)

    ffn_both = both_cores(ffn_in.astype(BF))
    gate_up = product(ffn_both, gate_up_half)
    hidden_low = swiglu(gate_up).astype(BF)
    ffn = sum_cores(product(hidden_low, down_half))
    branch_f, branch_f_pull = jax.vjp(branch_out, ffn, gain[3], gate_f)
    output = (hstate + branch_f).astype(BF)[None, :rows]

    ffn_grad, gain3_grad, gate_f_grad = branch_f_pull(upstream)
    ffn_grad_both = both_cores(ffn_grad.astype(BF))
    gate_up_low = swiglu_back(ffn_grad_both, down_half, gate_up)
    down_part = grad_of(hidden_low, ffn_grad_both)
    gate_up_part = grad_of(ffn_both, after(gate_up_low, down_part))
    down_part = reduce_dp(down_part)
    state_part, gain2_grad, scale_f_grad, shift_f_grad = ffn_in_pull(
        sum_cores(contract(gate_up_low, gate_up_half, 1, 1), gate_up_part)
    )
    state_grad = upstream + state_part
    proj_grad, gain1_grad, gate_a_grad = branch_a_pull(state_grad)
    proj_low = proj_grad.astype(BF)
    mixed_grad = contract(proj_low, mixer_full, 1, 1).astype(BF)
    ups = exchange_heads(simple_call(split_kernel, head_arrays(2), "split_heads", mixed_grad))
    mixer_part = grad_of(*column_split(mixed, after(proj_low, mixed_grad)))
    ups[0] = after(ups[0], mixer_part)
    gate_up_part = reduce_dp(after(gate_up_part, mixer_part))
    mixer_part = reduce_dp(mixer_part)
    ups[-1] = after(ups[-1], down_part)
    grads, dtexts, dgates = zip(*[
        attend_backward(
            qkv[i], text_own, bias, text_bias, gate_rows[i], ups[i], *attended[i][1:], i, 4 * half_slots
        )
        for i in range(heads)
    ])
    grads = list(grads)
    down_sum = Reduce(down_part)
    grads[0] = after(grads[0], down_sum.step())
    down_out = down_sum.finish()
    grads[-2] = after(grads[-2], down_out)
    down_out = down_out.astype(F32)
    grouped = exchange_back(grads)
    joint_low, rope_gain_grads = simple_call(
        functools.partial(ungroup_kernel, heads),
        [jax.ShapeDtypeStruct((slots, 3 * WIDTH), BF), jax.ShapeDtypeStruct((2, WIDTH), F32)],
        "ungroup_heads", *grouped, joint, rope_gains, cosine, sine,
    )
    joint_left, joint_right = column_split(normed_low, joint_low)
    piece = joint_right.shape[1] // 2
    joint_parts = [grad_of(joint_left, joint_right[:, p * piece : (p + 1) * piece]) for p in range(2)]
    joint_parts = [reduce_dp(after(part, gate_up_part, mixer_part)) for part in joint_parts]
    gate_up_sum = Reduce(gate_up_part)
    later_low = after(joint_low, gate_up_sum.step(joint_low))
    input_part, gain0_grad, scale_a_grad, shift_a_grad = normed_pull(
        contract(later_low, joint_full, 1, 1)
    )
    tokens_grad = (state_grad + input_part).astype(BF)[None, :rows]
    dtext = jnp.concatenate([v[:, :HEAD_DIM] for v in dtexts] + [v[:, HEAD_DIM:] for v in dtexts], axis=1)
    text_back = exchange(dtext.reshape(n_seq, text_rows, 2 * wide))
    text_key_grad, gain6_grad = text_key_pull(from_groups(text_back[:, :, :wide]).astype(F32))
    text_grad_rows = jnp.concatenate(
        [text_key_grad.astype(BF), from_groups(text_back[:, :, wide:])], axis=1
    )
    text_grad_all = lax.all_gather(after(text_grad_rows, joint_low), everyone, axis=0, tiled=True)
    text_grad = contract(flat_text, after(text_grad_all, joint_parts[1]), 0, 0)

    gates_own = jnp.concatenate([jnp.sum(v, axis=1) for v in dgates]) * (1.0 - own_gates * own_gates)
    gates_all = lax.dynamic_update_slice_in_dim(jnp.zeros((WIDTH,), F32), gates_own, first_head, 0)[None, :]
    pieces = [shift_a_grad, scale_a_grad, gate_a_grad, shift_f_grad, scale_f_grad, gate_f_grad]
    shared = [
        gain0_grad, gain1_grad, gain2_grad, gain3_grad, rope_gain_grads[0:1], rope_gain_grads[1:2], gain6_grad,
    ]
    tail = pieces + shared + [gates_all]
    tail = simple_call(
        pack_kernel, jax.ShapeDtypeStruct((-(-len(tail) // 8) * 8, WIDTH), F32), "pack_rows", *tail
    )
    gate_up_sum = gate_up_sum.finish(tail)
    joint_sums = [Reduce(after(part, tail)) for part in joint_parts]
    tails = [after(double(double(tail, "core", n_core), "z", n_z), gate_up_sum, joint_sums[0].step())]
    kept, received = [
        v.reshape(shard_rows, 2 * unit_blocks, 1, own_units)
        for v in trade(gate_up_sum)
    ]
    gate_up_out = by_core(kept, received, 2).reshape(shard_rows, -1).astype(F32)
    joint_sums = [part.finish(tails[0]) for part in joint_sums]
    joint_out = own_rows(jnp.concatenate(joint_sums, axis=1))
    mixer_out = own_rows(Reduce(after(mixer_part, tails[0])).finish())
    while len(tails) < n_dp:
        tails += list(swap(jnp.stack(tails), "dp", n_dp, len(tails)))
    count = len(pieces)
    total = tree([t[count:] for t in tails])
    gates_grad = total[gain_rows, :HEADS]
    gains_grad = lax.dynamic_slice_in_dim(total[:gain_rows], device * gain_width, gain_width, 1)
    mods_low = jnp.stack([t[:count].astype(BF).reshape(-1) for t in tails])
    cond_rows = jnp.concatenate(
        [lax.dynamic_slice_in_dim(soft_cond, dp ^ k, 1, 0) for k in range(n_dp)], axis=0
    )
    modulation_grad = contract(cond_rows, mods_low, 0, 0)
    bias_grad = lax.dynamic_slice_in_dim(
        jnp.sum(mods_low.astype(F32), axis=0), bias_start, bias_width, 0
    )
    return (
        output,
        tokens_grad,
        joint_out,
        mixer_out,
        gate_up_out,
        down_out,
        text_grad,
        modulation_grad,
        bias_grad,
        gains_grad,
        gates_grad,
    )


def solution(mesh):
    n_dp, n_seq = mesh.shape["dp"], mesh.shape["seq"]
    sizes = (n_dp, n_seq // 2, 2)
    split = Mesh(mesh.devices.reshape(sizes), ("dp", "z", "core"))
    seq, everyone = ("z", "core"), ("dp", "z", "core")
    token_spec, row_spec, column_spec = P("dp", seq, None), P(everyone, None), P(None, everyone)
    in_specs = (
        token_spec, column_spec, P(None, None, everyone), P(), P(), token_spec,
        row_spec, row_spec, row_spec, row_spec, row_spec, row_spec, P(everyone), column_spec, P(),
    )
    out_specs = (
        token_spec, token_spec, row_spec, row_spec, row_spec, row_spec, row_spec, row_spec,
        P(everyone), column_spec, P(),
    )
    return jax.shard_map(
        functools.partial(local, sizes), mesh=split, in_specs=in_specs, out_specs=out_specs, check_vma=False
    )
```

```python
import functools

import jax
import jax.numpy as jnp
from jax import lax
from jax.experimental import pallas as pl
from jax.experimental.pallas import tpu as pltpu
from jax.sharding import Mesh
from jax.sharding import PartitionSpec as P

HEADS = 24
HEAD_DIM = 64
TEXT = 256
WIDTH = HEADS * HEAD_DIM
EPS = 1e-06
NEG = -1e30
SCALE = float(HEAD_DIM) ** (-0.5)
LANES = 128
BF = jnp.bfloat16
F32 = jnp.float32
VMEM_BYTES = 56 << 20


def norm_rows(v, gain):
    return v * lax.rsqrt(jnp.mean(v * v, axis=-1, keepdims=True) + EPS) * gain


def modulate(v, gain, scale, shift):
    return norm_rows(v, gain) * (1.0 + scale) + shift


def branch_out(v, gain, gate):
    return gate * norm_rows(v, gain)


def swiglu(gate_up):
    half = gate_up.shape[-1] // 2
    return jax.nn.silu(gate_up[:, :half]) * gate_up[:, half:]


def product(left, right):
    return jnp.dot(left, right, preferred_element_type=F32)


def contract(left, right, left_dim, right_dim):
    return lax.dot_general(
        left, right, (((left_dim,), (right_dim,)), ((), ())), preferred_element_type=F32
    )


def split3(v):
    high = v.astype(BF)
    rest = v - high.astype(F32)
    mid = rest.astype(BF)
    return [high, mid, (rest - mid.astype(F32)).astype(BF)]


def extend(block, columns):
    rows = block.shape[0]
    fill = HEAD_DIM - len(columns)
    return jnp.concatenate([block] + list(columns) + [jnp.zeros((rows, fill), BF)], axis=1)


def unfold(v, start, period):
    return jnp.concatenate(
        [v[:, start : start + HEAD_DIM], v[:, period + start : period + start + HEAD_DIM]], axis=0
    )


def fold(parts):
    rows = parts[0].shape[0] // 2
    return jnp.concatenate([p[:rows] for p in parts] + [p[rows:] for p in parts], axis=1)


def spread_keys(index, qkv_ref, text_ref, bias_ref, text_bias_ref, outs, key_ones, value_ones):
    wide = text_ref.shape[1] // 2
    at = index * HEAD_DIM
    sources = (
        (unfold(qkv_ref, HEAD_DIM, 3 * HEAD_DIM), unfold(qkv_ref, 2 * HEAD_DIM, 3 * HEAD_DIM), bias_ref),
        (text_ref[:, at : at + HEAD_DIM], text_ref[:, wide + at : wide + at + HEAD_DIM], text_bias_ref),
    )
    for i, (keys, values, bias) in enumerate(sources):
        one = jnp.ones((keys.shape[0], 1), BF)
        outs[2 * i][...] = extend(keys, [bias[...]] + [one] * key_ones)
        outs[2 * i + 1][...] = extend(values, [one] * value_ones)


def attend_forward_kernel(
    index, qkv_ref, text_ref, bias_ref, text_bias_ref, gate_ref, q_ref,
    mixed_ref, own_ref, cross_ref, lse_ref, *spread
):
    @pl.when(pl.program_id(0) == 0)
    def _():
        spread_keys(index, qkv_ref, text_ref, bias_ref, text_bias_ref, spread, 0, 1)

    query = unfold(q_ref, 0, 3 * HEAD_DIM) * SCALE
    query = extend(query, [jnp.ones((query.shape[0], 1), BF)])

    def soft(keys, values):
        scores = contract(query, keys[...], 1, 1)
        high = jnp.max(scores, axis=1, keepdims=True)
        total = contract(jnp.exp(scores - high).astype(BF), values[...], 1, 0)
        mass = total[:, HEAD_DIM : HEAD_DIM + 1]
        return total[:, :HEAD_DIM] / mass, high + jnp.log(mass)

    own, own_lse = soft(spread[0], spread[1])
    cross, cross_lse = soft(spread[2], spread[3])
    own_ref[...] = fold([own])
    cross_ref[...] = fold([cross])
    mixed_ref[...] = fold([own + gate_ref[...] * cross]).astype(BF)
    lse_ref[...] = fold([own_lse, cross_lse])


def attend_backward_kernel(
    index, qkv_ref, text_ref, bias_ref, text_bias_ref, gate_ref, q_ref, up_ref, own_ref, cross_ref, lse_ref,
    grad_ref, dtext_ref, dgate_ref, *scratch
):
    spread, sums = scratch[:4], scratch[4:]
    step = pl.program_id(0)

    @pl.when(step == 0)
    def _():
        spread_keys(index, qkv_ref, text_ref, bias_ref, text_bias_ref, spread, 3, 3)
        for ref in sums + (dgate_ref,):
            ref[...] = jnp.zeros_like(ref)

    query = unfold(q_ref, 0, 3 * HEAD_DIM)
    one = jnp.ones((query.shape[0], 1), BF)
    up = unfold(up_ref, 0, HEAD_DIM)
    cross = unfold(cross_ref, 0, HEAD_DIM)
    up_float = up.astype(F32)
    up_cross = (gate_ref[...] * up_float).astype(BF)
    dgate_ref[...] += jnp.sum(up_float * cross, axis=0, keepdims=True)
    half = lse_ref.shape[0]
    lse = jnp.concatenate([lse_ref[:, 0:2], lse_ref[:, 2:4]], axis=0)

    def one_soft(upstream, row, spread_lse, keys, values, key_sum, value_sum):
        center = jnp.sum(row, axis=1, keepdims=True)
        left = extend(query * SCALE, [one] + [-part for part in split3(spread_lse)])
        weights = jnp.exp(contract(left, keys[...], 1, 1))
        left = extend(upstream, [-part for part in split3(center)])
        score_grad = (weights * contract(left, values[...], 1, 1)).astype(BF)
        weights = weights.astype(BF)
        key_sum[...] += contract(score_grad, query, 0, 0)
        value_sum[...] += contract(weights, upstream, 0, 0)
        return contract(score_grad, keys[...], 1, 0)[:, :HEAD_DIM]

    dq = one_soft(
        up, up_float * unfold(own_ref, 0, HEAD_DIM), lse[:, 0:1], spread[0], spread[1], sums[0], sums[1]
    )
    dq += one_soft(
        up_cross, up_cross.astype(F32) * cross, lse[:, 1:2], spread[2], spread[3], sums[2], sums[3]
    )
    dq = (dq * SCALE).astype(BF)
    here = pl.ds(pl.multiple_of(step * half, half), half)
    grad_ref[here, 0:HEAD_DIM] = dq[:half]
    grad_ref[here, 3 * HEAD_DIM : 4 * HEAD_DIM] = dq[half:]

    @pl.when(step == pl.num_programs(0) - 1)
    def _():
        slots = grad_ref.shape[0]
        both = jnp.concatenate([sums[0][...] * SCALE, sums[1][...]], axis=1).astype(BF)
        grad_ref[:, HEAD_DIM : 3 * HEAD_DIM] = both[:slots]
        grad_ref[:, 4 * HEAD_DIM :] = both[slots:]
        dtext_ref[...] = jnp.concatenate([sums[2][...] * SCALE, sums[3][...]], axis=1).astype(BF)


def whole_block(shape):
    return pl.BlockSpec(shape, lambda i: (0,) * len(shape), pipeline_mode=pl.Buffered(1))


def row_block(rows, columns):
    return pl.BlockSpec((rows, columns), lambda i: (i, 0))


def params():
    return pltpu.CompilerParams(vmem_limit_bytes=VMEM_BYTES)


def cost(flops, size, exps=0):
    return pl.CostEstimate(flops=int(flops), bytes_accessed=int(size), transcendentals=int(exps))


def attend_forward(qkv, text, bias, text_bias, gate, index, rows):
    half, words, head = qkv.shape[0], text.shape[0], HEAD_DIM
    slots = 2 * half
    pairs = slots * (slots + words)
    return pl.pallas_call(
        functools.partial(attend_forward_kernel, index),
        grid=(half // rows,),
        in_specs=[
            whole_block((half, 6 * head)), whole_block(text.shape), whole_block((slots, 1)),
            whole_block((words, 1)), whole_block((1, head)), row_block(rows, 6 * head),
        ],
        out_specs=[row_block(rows, 2 * head)] * 3 + [row_block(rows, 4)],
        out_shape=[
            jax.ShapeDtypeStruct((half, 2 * head), BF),
            jax.ShapeDtypeStruct((half, 2 * head), F32),
            jax.ShapeDtypeStruct((half, 2 * head), F32),
            jax.ShapeDtypeStruct((half, 4), F32),
        ],
        scratch_shapes=[pltpu.VMEM((n, 2 * head), BF) for n in (slots, slots, words, words)],
        compiler_params=params(),
        cost_estimate=cost(pairs * head * 16, slots * head * 18, pairs),
        name="attend_forward",
    )(qkv, text, bias, text_bias, gate, qkv)


def attend_backward(qkv, text, bias, text_bias, gate, up, own, cross, lse, index, rows):
    half, words, head = qkv.shape[0], text.shape[0], HEAD_DIM
    slots = 2 * half
    pairs = slots * (slots + words)
    return pl.pallas_call(
        functools.partial(attend_backward_kernel, index),
        grid=(half // rows,),
        in_specs=[
            whole_block((half, 6 * head)), whole_block(text.shape), whole_block((slots, 1)),
            whole_block((words, 1)), whole_block((1, head)), row_block(rows, 6 * head),
            row_block(rows, 2 * head), row_block(rows, 2 * head), row_block(rows, 2 * head), row_block(rows, 4),
        ],
        out_specs=[whole_block((half, 6 * head)), whole_block((words, 2 * head)), whole_block((1, head))],
        out_shape=[
            jax.ShapeDtypeStruct((half, 6 * head), BF),
            jax.ShapeDtypeStruct((words, 2 * head), BF),
            jax.ShapeDtypeStruct((1, head), F32),
        ],
        scratch_shapes=[pltpu.VMEM((n, 2 * head), BF) for n in (slots, slots, words, words)]
        + [pltpu.VMEM((n, head), F32) for n in (slots, slots, words, words)],
        compiler_params=params(),
        cost_estimate=cost(pairs * head * 40, slots * head * 26, pairs),
        name="attend_backward",
    )(qkv, text, bias, text_bias, gate, qkv, up, own, cross, lse)


def swap_halves(v):
    lane = lax.broadcasted_iota(jnp.int32, v.shape, 1)
    half = HEAD_DIM // 2
    return jnp.where(
        lane % HEAD_DIM < half, pltpu.roll(v, LANES - half, 1), pltpu.roll(v, half, 1)
    )


def tiles_of(v):
    return [v[:, t : t + LANES] for t in range(0, v.shape[1], LANES)]


def split_heads(parts, out_refs):
    heads, groups = len(out_refs), out_refs[0].shape[0]
    rows = parts[0].shape[0]
    for g in range(groups):
        for i in range(heads):
            at = (g * heads + i) * HEAD_DIM
            if at < WIDTH:
                out_refs[i][g] = fold([part[:, at : at + HEAD_DIM] for part in parts])
            else:
                out_refs[i][g] = jnp.zeros(out_refs[i].shape[1:], out_refs[i].dtype)


def join_heads(refs, which, count):
    groups, columns = refs[0].shape[0], []
    for g in range(groups):
        for i, ref in enumerate(refs):
            if (g * len(refs) + i) * HEAD_DIM < WIDTH:
                columns.append(unfold(ref.at[g], which * HEAD_DIM, count * HEAD_DIM))
    return jnp.concatenate(columns, axis=1)


def group_kernel(joint_ref, gains_ref, cos_ref, sin_ref, *out_refs):
    cosine, sine = cos_ref[...], sin_ref[...]
    parts = []
    for which in range(2):
        raw = joint_ref[:, which * WIDTH : (which + 1) * WIDTH]
        root = lax.rsqrt(jnp.mean(raw * raw, axis=1, keepdims=True) + EPS)
        scaled = raw * root * gains_ref[which : which + 1, :]
        turned = [tile * cosine + swap_halves(tile) * sine for tile in tiles_of(scaled)]
        parts.append(jnp.concatenate(turned, axis=1).astype(BF))
    parts.append(joint_ref[:, 2 * WIDTH :].astype(BF))
    split_heads(parts, out_refs)


def ungroup_kernel(heads, *refs):
    grad_refs = refs[:heads]
    joint_ref, gains_ref, cos_ref, sin_ref, out_ref, dgain_ref = refs[heads:]
    cosine, sine = cos_ref[...], sin_ref[...]
    for which in range(2):
        cut = slice(which * WIDTH, (which + 1) * WIDTH)
        grad = join_heads(grad_refs, which, 3).astype(F32)
        turned = [tile * cosine - swap_halves(tile) * sine for tile in tiles_of(grad)]
        grad = jnp.concatenate(turned, axis=1)
        raw = joint_ref[:, cut]
        root = lax.rsqrt(jnp.mean(raw * raw, axis=1, keepdims=True) + EPS)
        unit = raw * root
        dgain_ref[which : which + 1, :] = jnp.sum(grad * unit, axis=0, keepdims=True)
        grad = grad * gains_ref[which : which + 1, :]
        grad = root * (grad - unit * jnp.mean(grad * unit, axis=1, keepdims=True))
        out_ref[:, cut] = grad.astype(BF)
    out_ref[:, 2 * WIDTH :] = join_heads(grad_refs, 2, 3)


def split_kernel(value_ref, *out_refs):
    split_heads([value_ref[...]], out_refs)


def join_kernel(*refs):
    refs[-1][...] = join_heads(refs[:-1], 0, 1)


def swiglu_back_kernel(grad_ref, weight_ref, gate_ref, up_ref, out_ref):
    size, half = gate_ref.shape[1], out_ref.shape[1] // 2
    grad = contract(grad_ref[...], weight_ref[...], 1, 1)
    gate = gate_ref[...]
    sig = jax.nn.sigmoid(gate)
    at = pl.multiple_of(pl.program_id(0) * size, size)
    out_ref[:, pl.ds(at, size)] = (grad * up_ref[...] * (sig * (1.0 + gate * (1.0 - sig)))).astype(BF)
    out_ref[:, pl.ds(half + at, size)] = (grad * (gate * sig)).astype(BF)


def swiglu_back(grad, weight, gate_up):
    rows, width = grad.shape
    units = weight.shape[0]
    size = 2 * LANES
    count = units // size
    return pl.pallas_call(
        swiglu_back_kernel,
        grid=(count,),
        in_specs=[
            whole_block((rows, width)), row_block(size, width),
            pl.BlockSpec((rows, size), lambda i: (0, i)), pl.BlockSpec((rows, size), lambda i: (0, count + i)),
        ],
        out_specs=whole_block((rows, 2 * units)),
        out_shape=jax.ShapeDtypeStruct((rows, 2 * units), BF),
        compiler_params=params(),
        cost_estimate=cost(2 * rows * width * units, rows * units * 12 + units * width * 2, rows * units),
        name="swiglu_back",
    )(grad, weight, gate_up, gate_up)


def pack_kernel(*refs):
    out_ref = refs[-1]
    rows = [ref[...] for ref in refs[:-1]]
    rows.append(jnp.zeros((out_ref.shape[0] - len(rows), out_ref.shape[1]), F32))
    out_ref[...] = jnp.concatenate(rows, axis=0)


def simple_call(kernel, out_shape, name, *args):
    size = sum(a.size * a.dtype.itemsize for a in args)
    shapes = out_shape if isinstance(out_shape, list) else [out_shape]
    return pl.pallas_call(
        kernel,
        in_specs=[pl.BlockSpec(memory_space=pltpu.VMEM)] * len(args),
        out_specs=jax.tree.map(lambda _: pl.BlockSpec(memory_space=pltpu.VMEM), out_shape),
        out_shape=out_shape,
        compiler_params=params(),
        cost_estimate=cost(size * 8, size + sum(o.size * o.dtype.itemsize for o in shapes)),
        name=name,
    )(*args)


def local(
    sizes,
    tokens,
    condition,
    caption,
    caption_len,
    image_shape,
    cotangent,
    joint_weight,
    mixer_weight,
    gate_up_weight,
    down_weight,
    text_weight,
    modulation_weight,
    modulation_bias,
    norm_gains,
    head_gates,
):
    n_dp, n_z, n_core = sizes
    everyone = ("dp", "z", "core")
    seq = ("z", "core")
    n_seq = n_z * n_core
    heads = -(-HEADS // n_seq)
    wide = heads * HEAD_DIM
    spare = n_seq * heads - HEADS
    rows = tokens.shape[1]
    slots = -(-rows // 16) * 16
    dp = lax.axis_index("dp")
    core = lax.axis_index("core")
    z_index = lax.axis_index("z")
    seq_index = lax.axis_index(seq)
    device = lax.axis_index(everyone)

    def swap(v, axis, n, k):
        return lax.ppermute(v, axis, [(i, i ^ k) for i in range(n)])

    def tree(parts):
        while len(parts) > 1:
            parts = [parts[i] + parts[i + 1] for i in range(0, len(parts), 2)]
        return parts[0]

    def sum_over(v, axis, n):
        return tree([v] + [swap(v, axis, n, k) for k in range(1, n)])

    soft_cond = jax.nn.silu(condition).astype(BF)
    partial_mods = product(soft_cond, modulation_weight)
    bias_width = modulation_bias.shape[0]
    bias_start = device * bias_width
    with_bias = (
        lax.dynamic_slice_in_dim(partial_mods, bias_start, bias_width, 1) + modulation_bias[None, :]
    )
    partial_mods = lax.dynamic_update_slice_in_dim(partial_mods, with_bias, bias_start, 1)
    mods_width = partial_mods.shape[1]
    gain_rows, gain_width = norm_gains.shape
    own_gains = lax.dynamic_update_slice_in_dim(
        jnp.zeros((gain_rows, WIDTH), F32), norm_gains.astype(F32), device * gain_width, 1
    ).reshape(1, -1)

    def after(v, *others):
        return lax.optimization_barrier((v,) + others)[0]

    def shift_z(v, k):
        return lax.ppermute(v, "z", [(i, (i + k) % n_z) for i in range(n_z)])

    def place(full, part, index):
        return lax.dynamic_update_slice(full, part[None], (index,) + (0,) * part.ndim)


    def gather_line(shard):
        parts = [shift_z(shard, k) for k in range(1, n_z)]

        def arrive(*before):
            line = place(jnp.zeros((n_z,) + shard.shape, shard.dtype), shard, z_index)
            for k, part in enumerate(parts, 1):
                line = place(line, after(part, *before), (z_index - k) % n_z)
            return line.reshape(-1, shard.shape[1])

        return arrive

    class Gather:
        def __init__(self, shard):
            self.stack, self.offsets, self.next = shard[None], [0], n_z // 2
            self.send()

        def send(self):
            self.pending = swap(self.stack, "z", n_z, self.next) if self.next else None

        def step(self, *before):
            other = after(self.pending, *before)
            self.offsets = self.offsets + [offset ^ self.next for offset in self.offsets]
            self.stack = jnp.concatenate([self.stack, other], axis=0)
            self.next //= 2
            self.send()
            return self.stack

        def finish(self, *before):
            while self.next > 1:
                self.step(*before)
            count = len(self.offsets)
            last = after(self.pending, *before)
            line = jnp.zeros((n_z,) + last.shape[1:], last.dtype)
            for i, offset in enumerate(self.offsets):
                line = place(line, self.stack[i], z_index ^ offset)
                line = place(line, last[i], z_index ^ offset ^ self.next)
            return line.reshape(-1, last.shape[2])

    class Reduce:
        def __init__(self, part):
            self.line, self.next = part.reshape(n_z, -1, part.shape[1]), 1
            self.send()

        def send(self):
            if self.next < n_z:
                bit = (z_index // self.next) % 2
                pairs = self.line.reshape((-1, 2) + self.line.shape[1:])
                self.kept = lax.dynamic_index_in_dim(pairs, bit, 1, keepdims=False)
                sent = lax.dynamic_index_in_dim(pairs, 1 - bit, 1, keepdims=False)
                self.pending = swap(sent, "z", n_z, self.next)

        def step(self, *before):
            other = after(self.pending, *before)
            self.line = (self.kept.astype(F32) + other.astype(F32)).astype(BF)
            self.next *= 2
            self.send()
            return self.line

        def finish(self, *before):
            while self.next < n_z:
                self.step(*before)
            return self.line[0]

    def gather_dp(line):
        return lax.all_gather(line, "dp", axis=0, tiled=True)

    def gather_all(shard):
        if n_dp != 4:
            full = lax.all_gather(shard, everyone, axis=0, tiled=True)
            return lambda *before: lambda *before: full
        chunk, columns = shard.shape
        line_arrive = gather_line(shard)

        def first(*before):
            line = line_arrive(*before)
            empty = jnp.zeros((n_dp, n_z, n_core, chunk, columns), shard.dtype)
            line, empty = lax.optimization_barrier((line, empty))
            near = [swap(line, "dp", n_dp, k) for k in (1, 2)]

            def second(*before):
                half = line.shape[0] // 2
                by_x, by_y = [after(v, *before) for v in near]
                far = (swap(by_y[:half], "dp", n_dp, 1), swap(by_x[half:], "dp", n_dp, 2))
                full = empty
                parts = [(line, dp, 0), (by_x, dp ^ 1, 0), (by_y, dp ^ 2, 0)]
                parts += [(far[0], dp ^ 3, 0), (far[1], dp ^ 3, n_z // 2)]
                for part, index, start in parts:
                    for held, of_core in ((part, core), (swap(part, "core", n_core, 1), 1 - core)):
                        held = held.reshape(1, -1, 1, chunk, columns)
                        full = lax.dynamic_update_slice(full, held, (index, start, of_core, 0, 0))
                return full.reshape(-1, columns)

            second.line = line
            return second

        return first

    def reduce_dp(part):
        return lax.psum_scatter(part, "dp", scatter_dimension=0, tiled=True)

    def by_core(mine, other, axis):
        first = jnp.where(core == 0, mine, other)
        second = jnp.where(core == 0, other, mine)
        return jnp.concatenate([first, second], axis=axis)

    def column_split(left, right):
        half = right.shape[1] // n_core
        mine = lax.dynamic_slice_in_dim(right, core * half, half, 1)
        other = lax.dynamic_slice_in_dim(right, (1 - core) * half, half, 1)
        both_right = jnp.concatenate([mine, swap(other, "core", n_core, 1)], axis=0)
        return both_cores(left), both_right

    def both_cores(v):
        return jnp.concatenate([v, swap(v, "core", n_core, 1)], axis=0)

    def sum_cores(v, *before):
        return v[:slots] + after(swap(v[slots:], "core", n_core, 1), *before)

    def own_rows(part):
        return by_core(*trade(part.astype(BF)), 1).astype(F32)

    def core_columns(shard):
        half = shard.shape[1] // n_core
        mine = lax.dynamic_slice_in_dim(shard, core * half, half, 1)
        other = lax.dynamic_slice_in_dim(shard, (1 - core) * half, half, 1)
        return by_core(mine, swap(other, "core", n_core, 1), 0)

    def grad_of(left, right):
        return contract(left, right, 0, 0).astype(BF)

    def trade(part):
        count = part.shape[0] // n_core
        kept = lax.dynamic_slice_in_dim(part, core * count, count, 0)
        sent = lax.dynamic_slice_in_dim(part, (1 - core) * count, count, 0)
        return kept, swap(sent, "core", n_core, 1)

    flat_text = caption.reshape(-1, caption.shape[2])
    text_left, text_right = column_split(flat_text.T, text_weight)
    def halve(v):
        count = n_dp
        while count > 1:
            count //= 2
            bit = (dp // count) % 2
            kept = lax.dynamic_slice_in_dim(v, bit * count, count, 0)
            sent = lax.dynamic_slice_in_dim(v, (1 - bit) * count, count, 0)
            v = kept + swap(sent, "dp", n_dp, count)
        return v

    def double(v, axis, n):
        k = 1
        while k < n:
            v = v + swap(v, axis, n, k)
            k *= 2
        return v

    head_rows = jnp.concatenate(
        [partial_mods, jnp.broadcast_to(own_gains, (n_dp, own_gains.shape[1]))], axis=1
    )
    head_vector = double(double(halve(after(head_rows, text_right)), "core", n_core), "z", n_z)
    mods = head_vector[:, :mods_width]
    gains = head_vector[0, mods_width:].reshape(gain_rows, WIDTH)
    shift_a, scale_a, gate_a, shift_f, scale_f, gate_f = [
        mods[:, i * WIDTH : (i + 1) * WIDTH] for i in range(6)
    ]
    gain = [gains[i : i + 1] for i in range(gain_rows)]

    own_units = down_weight.shape[0]
    unit_blocks = n_dp * n_z
    shard_rows = gate_up_weight.shape[0]
    by_units = gate_up_weight.reshape(shard_rows, 2 * unit_blocks, n_core, own_units)


    def units_of(which):
        return lax.dynamic_index_in_dim(by_units, which, 2, keepdims=False).reshape(shard_rows, -1)

    gate_up_shard = by_core(units_of(core), swap(after(units_of(1 - core), mods), "core", n_core, 1), 0)
    text_part = grad_of(text_left, text_right)
    text_sum = lax.psum_scatter(text_part, ("dp", "z"), scatter_dimension=0, tiled=True)
    joint_near = gather_all(joint_weight)(text_part)
    joint_early = getattr(joint_near, "line", text_part)
    first_shard = jnp.concatenate([gate_up_shard, core_columns(after(mixer_weight, mods))], axis=1)
    first_line = Gather(after(first_shard, joint_early))
    first_early = first_line.step()

    pad = ((0, slots - rows), (0, 0))
    xfloat = jnp.pad(tokens[0], pad).astype(F32)
    upstream = jnp.pad(cotangent[0], pad).astype(F32)
    normed_in, normed_pull = jax.vjp(modulate, xfloat, gain[0], scale_a, shift_a)
    normed_low = normed_in.astype(BF)
    joint_full = joint_near(normed_low, first_early)
    joint = product(normed_low, joint_full)
    def to_groups(parts):
        count = parts[0].shape[0]
        spread = []
        for part in parts:
            part = jnp.pad(part, ((0, 0), (0, spare * HEAD_DIM)))
            spread.append(part.reshape(count, n_seq, wide).transpose(1, 0, 2))
        return jnp.concatenate(spread, axis=2)

    def from_groups(part):
        part = part.transpose(1, 0, 2)
        return part.reshape(part.shape[0], n_seq * wide)[:, :WIDTH]

    def exchange(v):
        return lax.all_to_all(v, seq, 0, 0, tiled=True)

    lane = jnp.arange(LANES)
    freq = jnp.exp((lane % (HEAD_DIM // 2)).astype(F32) * (-jnp.log(10000.0) / (HEAD_DIM // 2)))
    angle = (seq_index * rows + jnp.arange(slots)).astype(F32)[:, None] * freq[None, :]
    cosine = jnp.cos(angle)
    sine = jnp.sin(angle) * jnp.where(lane % HEAD_DIM < HEAD_DIM // 2, -1.0, 1.0)[None, :]
    rope_gains = gains[4:6]
    half_slots = slots // 2

    def head_arrays(columns):
        return [jax.ShapeDtypeStruct((n_seq, half_slots, columns * HEAD_DIM), BF)] * heads

    def exchange_heads(arrays):
        return [exchange(v).reshape(n_seq * half_slots, -1) for v in arrays]

    def exchange_back(arrays):
        return [exchange(v.reshape(n_seq, half_slots, -1)) for v in arrays]

    sent = simple_call(group_kernel, head_arrays(6), "group_heads", joint, rope_gains, cosine, sine)
    sent = list(sent)
    first_line = first_line.finish(joint)
    sent[0] = after(sent[0], first_line)
    split_at = gate_up_shard.shape[1]
    mixer_half = gather_dp(first_line[:, split_at:])
    gate_up_half = gather_dp(first_line[:, :split_at])
    down_line = Gather(after(down_weight, first_line))
    text_raw = own_rows(after(text_sum, sent[0]))
    text_rows = text_raw.shape[0]
    text_keys, text_key_pull = jax.vjp(norm_rows, text_raw[:, :WIDTH], gain[6])
    text_own = exchange(
        to_groups([text_keys.astype(BF), text_raw[:, WIDTH:].astype(BF)])
    ).reshape(n_seq * text_rows, 2 * wide)

    sent[1] = after(sent[1], text_own)
    qkv = exchange_heads(sent)
    mixer_full = by_core(mixer_half, swap(mixer_half, "core", n_core, 1), 1)
    down_half = gather_dp(down_line.finish(qkv[0]))
    slot = jnp.arange(n_seq * slots)
    side, line = slot // (n_seq * half_slots), slot % (n_seq * half_slots)
    within = side * half_slots + line % half_slots
    shape_row = image_shape[dp]
    valid = shape_row[0] * (shape_row[1] + 1)
    live = (within < rows) & ((line // half_slots) * rows + within < valid)
    bias = jnp.where(live, 0.0, NEG).astype(BF)[:, None]
    text_bias = jnp.where(jnp.arange(TEXT) < caption_len[dp], 0.0, NEG).astype(BF)[:, None]
    tanh_gates = jnp.tanh(head_gates)
    first_head = seq_index * heads
    own_gates = lax.dynamic_slice_in_dim(jnp.pad(tanh_gates, (0, spare)), first_head, heads, 0)
    gate_rows = [jnp.broadcast_to(own_gates[i : i + 1, None], (1, HEAD_DIM)) for i in range(heads)]
    attended = [
        attend_forward(qkv[i], text_own, bias, text_bias, gate_rows[i], i, 4 * half_slots)
        for i in range(heads)
    ]
    token_shape = jax.ShapeDtypeStruct((slots, WIDTH), BF)
    mixed = simple_call(
        join_kernel, token_shape, "join_heads", *exchange_back([v[0] for v in attended])
    )
    proj = product(mixed, mixer_full)
    branch_a, branch_a_pull = jax.vjp(branch_out, proj, gain[1], gate_a)
    hstate = xfloat + branch_a
    ffn_in, ffn_in_pull = jax.vjp(modulate, hstate, gain[2], scale_f, shift_f)

    ffn_both = both_cores(ffn_in.astype(BF))
    gate_up = product(ffn_both, gate_up_half)
    hidden_low = swiglu(gate_up).astype(BF)
    ffn = sum_cores(product(hidden_low, down_half))
    branch_f, branch_f_pull = jax.vjp(branch_out, ffn, gain[3], gate_f)
    output = (hstate + branch_f).astype(BF)[None, :rows]

    ffn_grad, gain3_grad, gate_f_grad = branch_f_pull(upstream)
    ffn_grad_both = both_cores(ffn_grad.astype(BF))
    gate_up_low = swiglu_back(ffn_grad_both, down_half, gate_up)
    down_part = grad_of(hidden_low, ffn_grad_both)
    gate_up_part = grad_of(ffn_both, after(gate_up_low, down_part))
    down_part = reduce_dp(down_part)
    state_part, gain2_grad, scale_f_grad, shift_f_grad = ffn_in_pull(
        sum_cores(contract(gate_up_low, gate_up_half, 1, 1), gate_up_part)
    )
    state_grad = upstream + state_part
    proj_grad, gain1_grad, gate_a_grad = branch_a_pull(state_grad)
    proj_low = proj_grad.astype(BF)
    mixed_grad = contract(proj_low, mixer_full, 1, 1).astype(BF)
    ups = exchange_heads(simple_call(split_kernel, head_arrays(2), "split_heads", mixed_grad))
    mixer_part = grad_of(*column_split(mixed, after(proj_low, mixed_grad)))
    ups[0] = after(ups[0], mixer_part)
    gate_up_part = reduce_dp(after(gate_up_part, mixer_part))
    mixer_part = reduce_dp(mixer_part)
    ups[-1] = after(ups[-1], down_part)
    grads, dtexts, dgates = zip(*[
        attend_backward(
            qkv[i], text_own, bias, text_bias, gate_rows[i], ups[i], *attended[i][1:], i, 4 * half_slots
        )
        for i in range(heads)
    ])
    grads = list(grads)
    down_sum = Reduce(down_part)
    grads[0] = after(grads[0], down_sum.step())
    down_out = down_sum.finish()
    grads[-2] = after(grads[-2], down_out)
    down_out = down_out.astype(F32)
    grouped = exchange_back(grads)
    joint_low, rope_gain_grads = simple_call(
        functools.partial(ungroup_kernel, heads),
        [jax.ShapeDtypeStruct((slots, 3 * WIDTH), BF), jax.ShapeDtypeStruct((2, WIDTH), F32)],
        "ungroup_heads", *grouped, joint, rope_gains, cosine, sine,
    )
    joint_left, joint_right = column_split(normed_low, joint_low)
    joint_parts = [grad_of(joint_left, joint_right)]
    joint_parts = [reduce_dp(after(part, gate_up_part, mixer_part)) for part in joint_parts]
    gate_up_sum = Reduce(gate_up_part)
    later_low = after(joint_low, gate_up_sum.step(joint_low))
    input_part, gain0_grad, scale_a_grad, shift_a_grad = normed_pull(
        contract(later_low, joint_full, 1, 1)
    )
    tokens_grad = (state_grad + input_part).astype(BF)[None, :rows]
    dtext = jnp.concatenate([v[:, :HEAD_DIM] for v in dtexts] + [v[:, HEAD_DIM:] for v in dtexts], axis=1)
    text_back = exchange(dtext.reshape(n_seq, text_rows, 2 * wide))
    text_key_grad, gain6_grad = text_key_pull(from_groups(text_back[:, :, :wide]).astype(F32))
    text_grad_rows = jnp.concatenate(
        [text_key_grad.astype(BF), from_groups(text_back[:, :, wide:])], axis=1
    )
    text_grad_all = lax.all_gather(after(text_grad_rows, joint_low), everyone, axis=0, tiled=True)
    text_grad = contract(flat_text, after(text_grad_all, joint_parts[-1]), 0, 0)

    gates_own = jnp.concatenate([jnp.sum(v, axis=1) for v in dgates]) * (1.0 - own_gates * own_gates)
    gates_all = lax.dynamic_update_slice_in_dim(jnp.zeros((WIDTH,), F32), gates_own, first_head, 0)[None, :]
    pieces = [shift_a_grad, scale_a_grad, gate_a_grad, shift_f_grad, scale_f_grad, gate_f_grad]
    shared = [
        gain0_grad, gain1_grad, gain2_grad, gain3_grad, rope_gain_grads[0:1], rope_gain_grads[1:2], gain6_grad,
    ]
    tail = pieces + shared + [gates_all]
    tail = simple_call(
        pack_kernel, jax.ShapeDtypeStruct((-(-len(tail) // 8) * 8, WIDTH), F32), "pack_rows", *tail
    )
    gate_up_sum = gate_up_sum.finish(tail)
    joint_sums = [Reduce(after(part, tail)) for part in joint_parts]
    tails = [after(double(double(tail, "core", n_core), "z", n_z), gate_up_sum, joint_sums[0].step())]
    kept, received = [
        v.reshape(shard_rows, 2 * unit_blocks, 1, own_units)
        for v in trade(gate_up_sum)
    ]
    gate_up_out = by_core(kept, received, 2).reshape(shard_rows, -1).astype(F32)
    joint_sums = [part.finish(tails[0]) for part in joint_sums]
    joint_out = own_rows(jnp.concatenate(joint_sums, axis=1))
    mixer_out = own_rows(Reduce(after(mixer_part, tails[0])).finish())
    while len(tails) < n_dp:
        tails += list(swap(jnp.stack(tails), "dp", n_dp, len(tails)))
    count = len(pieces)
    total = tree([t[count:] for t in tails])
    gates_grad = total[gain_rows, :HEADS]
    gains_grad = lax.dynamic_slice_in_dim(total[:gain_rows], device * gain_width, gain_width, 1)
    mods_low = jnp.stack([t[:count].astype(BF).reshape(-1) for t in tails])
    cond_rows = jnp.concatenate(
        [lax.dynamic_slice_in_dim(soft_cond, dp ^ k, 1, 0) for k in range(n_dp)], axis=0
    )
    modulation_grad = contract(cond_rows, mods_low, 0, 0)
    bias_grad = lax.dynamic_slice_in_dim(
        jnp.sum(mods_low.astype(F32), axis=0), bias_start, bias_width, 0
    )
    return (
        output,
        tokens_grad,
        joint_out,
        mixer_out,
        gate_up_out,
        down_out,
        text_grad,
        modulation_grad,
        bias_grad,
        gains_grad,
        gates_grad,
    )


def solution(mesh):
    n_dp, n_seq = mesh.shape["dp"], mesh.shape["seq"]
    sizes = (n_dp, n_seq // 2, 2)
    split = Mesh(mesh.devices.reshape(sizes), ("dp", "z", "core"))
    seq, everyone = ("z", "core"), ("dp", "z", "core")
    token_spec, row_spec, column_spec = P("dp", seq, None), P(everyone, None), P(None, everyone)
    in_specs = (
        token_spec, column_spec, P(None, None, everyone), P(), P(), token_spec,
        row_spec, row_spec, row_spec, row_spec, row_spec, row_spec, P(everyone), column_spec, P(),
    )
    out_specs = (
        token_spec, token_spec, row_spec, row_spec, row_spec, row_spec, row_spec, row_spec,
        P(everyone), column_spec, P(),
    )
    return jax.shard_map(
        functools.partial(local, sizes), mesh=split, in_specs=in_specs, out_specs=out_specs, check_vma=False
    )
```
